128 devices in a mesh: replica: 16 (over y, z_lo, core), tensor: 8 (over x, z_hi).
Axes of the slice: x: 4, y: 4, z: 4 (z_hi: 2, z_lo: 2; z = z_hi * 2 + z_lo), core: 2. Of those that a mesh axis runs over, the one named last changes fastest.
Arguments:
- hidden: bfloat16 [24576, 5120], P(('replica', 'tensor')), may hold values from -6 to 6
- w_key: float32 [16, 5120, 1024], P('replica', None, 'tensor'), may hold values from -0.078125 to 0.078125
- w_value: float32 [16, 5120, 1024], P('replica', None, 'tensor'), may hold values from -0.078125 to 0.078125
- moment_key: float32 [16, 5120, 1024], P('replica', None, 'tensor'), may hold values from -60 to 60
- moment_value: float32 [16, 5120, 1024], P('replica', None, 'tensor'), may hold values from -60 to 60
- second_key: float32 [16, 5120, 1024], P('replica', None, 'tensor'), may hold values from 100 to 1000
- second_value: float32 [16, 5120, 1024], P('replica', None, 'tensor'), may hold values from 100 to 1000
- grad_keys: bfloat16 [24576, 1024], P('replica', 'tensor'), may hold values from -6 to 6
- grad_values: bfloat16 [24576, 1024], P('replica', 'tensor'), may hold values from -6 to 6
- seed_panels: int32 [2, 1024, 32], P(None, 'tensor'), may hold values from -2 to 2
- partner: int32 [16], replicated, may hold values from 0 to 15, as said below
Outputs:
- keys: bfloat16 [24576, 1024], P('replica', 'tensor')
- values: bfloat16 [24576, 1024], P('replica', 'tensor')
- input_grad: bfloat16 [24576, 5120], P(('replica', 'tensor'))
- new_key: float32 [16, 5120, 1024], P('replica', None, 'tensor')
- new_value: float32 [16, 5120, 1024], P('replica', None, 'tensor')
The draws below stay inside these ranges and needn't reach their ends.
Inputs may be any that keep to these rules, and one draw needn't show every extreme that they name: partner[partner[r]] = r and partner[r] != r for every replica r.
All inputs are finite; a program needn't handle non-finite values.
Results may differ from the reference program's by a relative error of at most 0.012.
Values may be sent and summed in bfloat16 or wider, within the bound.
A program may use at most 192 MiB of HBM per device.

```python
import math
import jax
import jax.numpy as jnp
from jax import lax

D = 5120
KVD = 1024
RANK = 32
REPLICAS = 16
ALL_ROWS = 24576
HEAD_COLS = 128
N_TENSOR = 8


def draw_partner(key, part):
    order = jax.random.permutation(key, REPLICAS)
    firsts = order[0::2].astype(jnp.int32)
    seconds = order[1::2].astype(jnp.int32)
    matched = jnp.zeros((REPLICAS,), jnp.int32)
    matched = matched.at[firsts].set(seconds)
    return matched.at[seconds].set(firsts)


def plant(values, key, low, high):
    extent = values.shape
    index_at = [jax.random.randint(jax.random.fold_in(key, axis), (), 0, extent[axis]) for axis in range(len(extent))]
    values = values.at[tuple(index_at)].set(low)
    longest = extent.index(max(extent))
    index_at[longest] = (index_at[longest] + 1) % extent[longest]
    return values.at[tuple(index_at)].set(high)


def block_levels(own_key, extent, cuts, least, largest):
    factor_of, own = 1.0, jax.random.fold_in(own_key, 6)
    for position, parts in cuts:
        draws = jnp.exp(jax.random.uniform(jax.random.fold_in(own, position), (parts,), jnp.float32, least / len(cuts), largest / len(cuts)))
        factor_of = factor_of * jnp.repeat(draws, extent[position] // parts).reshape([-1 if axis == position else 1 for axis in range(len(extent))])
    return factor_of


def normal_values(own_key, shape, spread, bound, cuts=(), kind=jnp.bfloat16):
    gain = block_levels(own_key, shape, cuts, -0.22, 0.18) if cuts else 1.0
    array = jax.random.normal(own_key, shape, jnp.float32) * spread * gain
    return jnp.minimum(jnp.maximum(array, -bound), bound).astype(kind)


def setup_inputs(seed: int = 0) -> dict:
    key_list = jax.random.split(jax.random.key(seed), 12)
    hidden = normal_values(key_list[0], (ALL_ROWS, D), 1.0, 6.0, ((0, 128),))
    w_key = normal_values(key_list[1], (REPLICAS, D, KVD), D ** -0.5, 0.078125, ((0, 16), (2, 8)), jnp.float32)
    w_value = normal_values(key_list[2], (REPLICAS, D, KVD), D ** -0.5, 0.078125, ((0, 16), (2, 8)), jnp.float32)
    moment_key = normal_values(key_list[3], (REPLICAS, D, KVD), 10.0, 60.0, ((0, 16), (2, 8)), jnp.float32)
    moment_value = normal_values(key_list[4], (REPLICAS, D, KVD), 10.0, 60.0, ((0, 16), (2, 8)), jnp.float32)
    second_key = jnp.clip(jnp.exp(math.log(1000.0) - 2.3025851 * jax.random.uniform(key_list[5], (REPLICAS, D, KVD), jnp.float32) ** block_levels(key_list[5], (REPLICAS, D, KVD), ((0, 16), (2, 8)), -0.2, 0.2)), 100.0, 1000.0)
    second_value = jnp.clip(jnp.exp(math.log(1000.0) - 2.3025851 * jax.random.uniform(key_list[6], (REPLICAS, D, KVD), jnp.float32) ** block_levels(key_list[6], (REPLICAS, D, KVD), ((0, 16), (2, 8)), -0.2, 0.2)), 100.0, 1000.0)
    grad_keys = normal_values(key_list[7], (ALL_ROWS, KVD), 1.0, 6.0, ((0, 16), (1, 8)))
    grad_values = normal_values(key_list[8], (ALL_ROWS, KVD), 1.0, 6.0, ((0, 16), (1, 8)))
    seed_panels = plant(jax.random.randint(key_list[9], (2, KVD, RANK), -2, 3), jax.random.fold_in(key_list[9], 1), -2, 2).astype(jnp.int32)
    partner = draw_partner(jax.random.fold_in(key_list[11], 71), 0)
    return {"hidden": hidden, "w_key": w_key, "w_value": w_value, "moment_key": moment_key, "moment_value": moment_value, "second_key": second_key, "second_value": second_value, "grad_keys": grad_keys, "grad_values": grad_values, "seed_panels": seed_panels, "partner": partner}


beta_one = 0.9
beta_two = 0.95
epsilon = 1e-08
learn_rate = 0.06
decay_rate = 0.1
step_count = 100.0

def adam_step(weight, moment, second, gradient):
    moment_new = beta_one * moment + (1.0 - beta_one) * gradient
    second_new = beta_two * second + (1.0 - beta_two) * gradient * gradient
    first_hat = moment_new / (1.0 - beta_one ** step_count)
    second_hat = second_new / (1.0 - beta_two ** step_count)
    return weight - learn_rate * (first_hat / (jnp.sqrt(second_hat) + epsilon) + decay_rate * weight)

def orthonormal(panel):
    gram_matrix = jnp.einsum('mds,mdt->mst', panel, panel, precision=lax.Precision.HIGHEST)
    lower_factor = jnp.linalg.cholesky(gram_matrix)
    return lax.linalg.triangular_solve(lower_factor, panel, left_side=False, lower=True, transpose_a=True)

def gossip(adapted, start_panel, partner):
    start_float = start_panel.astype(jnp.float32)
    panel_own = jnp.einsum('rdc,cs->rds', adapted, start_float, precision=lax.Precision.HIGHEST)
    panel_diff = panel_own - panel_own[partner]
    basis_panel = orthonormal(panel_diff)
    side_panel = jnp.einsum('rdc,rds->rcs', adapted, basis_panel, precision=lax.Precision.HIGHEST)
    side_diff = side_panel + side_panel[partner]
    return adapted - 0.5 * jnp.einsum('rds,rcs->rdc', basis_panel, side_diff, precision=lax.Precision.HIGHEST)

def reference(hidden, w_key, w_value, moment_key, moment_value, second_key, second_value, grad_keys, grad_values, seed_panels, partner):
    replica_count = w_key.shape[0]
    row_count = hidden.shape[0] // replica_count
    hidden_rows = hidden.reshape(replica_count, row_count, D).astype(jnp.float32)
    dkey_rows = grad_keys.reshape(replica_count, row_count, KVD).astype(jnp.float32)
    dvalue_rows = grad_values.reshape(replica_count, row_count, KVD).astype(jnp.float32)
    key_bf = w_key.astype(jnp.bfloat16)
    value_bf = w_value.astype(jnp.bfloat16)
    keys = jnp.einsum('rnd,rdc->rnc', hidden_rows, key_bf.astype(jnp.float32)).astype(jnp.bfloat16)
    values = jnp.einsum('rnd,rdc->rnc', hidden_rows, value_bf.astype(jnp.float32)).astype(jnp.bfloat16)
    grad_key = jnp.einsum('rnd,rnc->rdc', hidden_rows, dkey_rows)
    grad_value = jnp.einsum('rnd,rnc->rdc', hidden_rows, dvalue_rows)

    def replica_input(items):
        dkey_one, dvalue_one, wkey_one, wvalue_one = items
        dkey_three = dkey_one.reshape(row_count, N_TENSOR, HEAD_COLS)
        dvalue_three = dvalue_one.reshape(row_count, N_TENSOR, HEAD_COLS)
        wkey_three = wkey_one.astype(jnp.float32).reshape(D, N_TENSOR, HEAD_COLS)
        wvalue_three = wvalue_one.astype(jnp.float32).reshape(D, N_TENSOR, HEAD_COLS)
        terms = jnp.einsum('ntc,dtc->tnd', dkey_three, wkey_three) + jnp.einsum('ntc,dtc->tnd', dvalue_three, wvalue_three)
        rounded = lax.optimization_barrier(terms.astype(jnp.bfloat16))
        return lax.optimization_barrier(jnp.sum(rounded.astype(jnp.float32), axis=0)).astype(jnp.bfloat16)
    input_grad = lax.map(replica_input, (dkey_rows, dvalue_rows, key_bf, value_bf))
    adapted_key = adam_step(w_key, moment_key, second_key, grad_key)
    adapted_value = adam_step(w_value, moment_value, second_value, grad_value)
    new_key = gossip(adapted_key, seed_panels[0], partner)
    new_value = gossip(adapted_value, seed_panels[1], partner)
    return (keys.reshape(ALL_ROWS, KVD), values.reshape(ALL_ROWS, KVD), input_grad.reshape(ALL_ROWS, D), new_key, new_value)
```

```python
import functools
import jax
import jax.numpy as jnp
from jax import lax
from jax.experimental import pallas as pl
from jax.experimental.pallas import tpu as pltpu
from jax.sharding import PartitionSpec as P

MESH = pl.DeviceIdType.MESH
beta_one = 0.9
beta_two = 0.95
epsilon = 1e-08
learn_rate = 0.06
decay_rate = 0.1
step_count = 100.0

NC = 5
CH = 1024
RB = 192
HR = 96
HC = 128
bf16 = jnp.bfloat16
f32 = jnp.float32


def slots(x):
    return (x, lax.rem(x + 3, 4), lax.rem(x + 1, 4), lax.rem(x + 2, 4))


def dot_tn(a, b):
    return lax.dot_general(a, b, (((0,), (0,)), ((), ())), preferred_element_type=f32)


def dot_nt(a, b):
    return lax.dot_general(a, b, (((1,), (1,)), ((), ())), preferred_element_type=f32)


def dot_nn(a, b):
    return lax.dot_general(a, b, (((1,), (0,)), ((), ())), preferred_element_type=f32)


def first_kernel(
    h_ref, wk_ref, wv_ref, mk_ref, mv_ref, sk_ref, sv_ref, gk_ref, gv_ref, st_ref,
    keys_o, vals_o, ig_o, ad_o, pan_o,
    hz, wp, dk, gown, gsend, grecv, wcv, adin, ts, trh, trf, kacc, kst, pan,
    lh_s, hs_s, hr_s, fs_s, fr_s, ldk_s, dks_s, dkr_s, lw_s, ws_s, wr_s, gs_s, gr_s,
    lad_s, t1s_s, t1r_s, t2s_s, t2r_s, ko_s, ks_s, kr_s, out_s,
):
    r = lax.axis_index("replica")
    t = lax.axis_index("tensor")
    x = t // 2
    z = lax.rem(t, 2)
    right = (r, lax.rem(x + 1, 4) * 2 + z)
    left = (r, lax.rem(x + 3, 4) * 2 + z)
    pair = (r, x * 2 + (1 - z))
    sl = slots(x)
    g_refs = (gk_ref, gv_ref)
    w_refs = (wk_ref, wv_ref)
    ad_refs = ((wk_ref, wv_ref), (mk_ref, mv_ref), (sk_ref, sv_ref))

    def rcopy(src, dst, ssem, rsem, dev):
        return pltpu.make_async_remote_copy(
            src_ref=src, dst_ref=dst, send_sem=ssem, recv_sem=rsem,
            device_id=dev, device_id_type=MESH,
        )

    def lcopy(src, dst, sem):
        return pltpu.make_async_copy(src, dst, sem)

    dk_loc = [
        lcopy(g_refs[a].at[sl[s], z], dk.at[0, s, :, pl.ds(a * HC, HC)], ldk_s.at[s, a])
        for s in range(4) for a in range(2)
    ]
    h_loc = [lcopy(h_ref.at[:, pl.ds(c * CH, CH)], hz.at[c, 0], lh_s.at[c]) for c in range(NC)]
    w_loc = [
        [lcopy(w_refs[a].at[0, pl.ds(c * CH, CH)], wcv.at[c % 2, a], lw_s.at[c % 2, a]) for a in range(2)]
        for c in range(NC)
    ]
    ad_loc = [
        [
            lcopy(ad_refs[k][a].at[0, pl.ds(c * CH, CH)], adin.at[c % 2, k, a], lad_s.at[c % 2, k, a])
            for k in range(3) for a in range(2)
        ]
        for c in range(NC)
    ]
    for c in (0, 1):
        for cp in w_loc[c]:
            cp.start()
    for cp in dk_loc:
        cp.start()
    for cp in h_loc:
        cp.start()

    barrier = pltpu.get_barrier_semaphore()
    for dev in (right, left, pair):
        pl.semaphore_signal(barrier, inc=1, device_id=dev, device_id_type=MESH)
    pl.semaphore_wait(barrier, 3)

    h_r = [rcopy(h_ref.at[:, pl.ds(c * CH, CH)], hz.at[c, 1], hs_s.at[c, 0], hr_s.at[c, 0], right) for c in range(NC)]
    h_l = [rcopy(h_ref.at[:, pl.ds(c * CH, CH)], hz.at[c, 2], hs_s.at[c, 1], hr_s.at[c, 1], left) for c in range(NC)]
    f_r = [rcopy(hz.at[c, 1, pl.ds(0, HR)], hz.at[c, 3, pl.ds(0, HR)], fs_s.at[c, 0], fr_s.at[c, 0], right) for c in range(NC)]
    f_l = [rcopy(hz.at[c, 2, pl.ds(HR, HR)], hz.at[c, 3, pl.ds(HR, HR)], fs_s.at[c, 1], fr_s.at[c, 1], left) for c in range(NC)]
    dk_x = [
        rcopy(g_refs[a].at[sl[s], 1 - z], dk.at[1, s, :, pl.ds(a * HC, HC)], dks_s.at[s, a], dkr_s.at[s, a], pair)
        for s in range(4) for a in range(2)
    ]
    w_x = [rcopy(wp.at[c, 0], wp.at[c, 1], ws_s.at[c], wr_s.at[c], pair) for c in range(NC)]
    g_x = [rcopy(gsend.at[c], grecv.at[c], gs_s.at[c], gr_s.at[c], pair) for c in range(NC)]
    t1_r = [rcopy(ts.at[c, 3, pl.ds(0, HR)], trh.at[c, 0], t1s_s.at[c, 0], t1r_s.at[c, 0], right) for c in range(NC)]
    t1_l = [rcopy(ts.at[c, 3, pl.ds(HR, HR)], trh.at[c, 1], t1s_s.at[c, 1], t1r_s.at[c, 1], left) for c in range(NC)]
    t2_r = [rcopy(ts.at[c, 2], trf.at[c, 0], t2s_s.at[c, 0], t2r_s.at[c, 0], right) for c in range(NC)]
    t2_l = [rcopy(ts.at[c, 1], trf.at[c, 1], t2s_s.at[c, 1], t2r_s.at[c, 1], left) for c in range(NC)]

    def send_h(c):
        h_r[c].start()
        h_l[c].start()

    def convert_w(c):
        for cp in w_loc[c]:
            cp.wait()

        @pl.loop(0, CH // 256)
        def _(i):
            rows = pl.ds(i * 256, 256)
            for a in range(2):
                wp[c, 0, rows, pl.ds(a * HC, HC)] = wcv[c % 2, a, rows].astype(bf16)

        if c + 2 < NC:
            for cp in w_loc[c + 2]:
                cp.start()

    def forward_h(c):
        h_r[c].wait_recv()
        f_r[c].start()
        h_l[c].wait_recv()
        f_l[c].start()

    def grads(c):
        h_loc[c].wait()
        f_r[c].wait_recv()
        f_l[c].wait_recv()

        @pl.loop(0, CH // 256)
        def _(i):
            cols = pl.ds(pl.multiple_of(i * 256, 256), 256)
            rows = pl.ds(i * 256, 256)
            lhs = hz[c, :, :, cols].reshape(4 * RB, 256)
            gsend[c, rows] = dot_tn(lhs, dk[1].reshape(4 * RB, 2 * HC)).astype(bf16)
            gown[c, rows] = dot_tn(lhs, dk[0].reshape(4 * RB, 2 * HC))

        g_x[c].start()

    def produce(c):
        for s in range(4):
            for p in range(2):
                add = dot_nn(hz[c, s], wp[c, p])
                if c == 0:
                    kacc[p, s] = add
                elif c < NC - 1:
                    kacc[p, s] = kacc[p, s] + add
                else:
                    kst[p, s] = (kacc[p, s] + add).astype(bf16)

    def term(c, s):
        @pl.loop(0, CH // 256)
        def _(i):
            cols = pl.ds(pl.multiple_of(i * 256, 256), 256)
            rows = pl.ds(i * 256, 256)
            ts[c, s, :, cols] = (
                dot_nt(dk[0, s], wp[c, 0, rows]) + dot_nt(dk[1, s], wp[c, 1, rows])
            ).astype(bf16)

    def terms_first(c):
        w_x[c].wait_recv()
        term(c, 3)
        t1_r[c].start()
        t1_l[c].start()
        term(c, 2)
        term(c, 1)
        term(c, 0)

    def terms_second(c):
        t1_r[c].wait_recv()
        ts[c, 2, pl.ds(0, HR)] = (ts[c, 2, pl.ds(0, HR)].astype(f32) + trh[c, 0].astype(f32)).astype(bf16)
        t2_r[c].start()
        t1_l[c].wait_recv()
        ts[c, 1, pl.ds(HR, HR)] = (ts[c, 1, pl.ds(HR, HR)].astype(f32) + trh[c, 1].astype(f32)).astype(bf16)
        t2_l[c].start()

    ig_cp = [lcopy(ts.at[c, 0], ig_o.at[:, pl.ds(c * CH, CH)], out_s.at[c]) for c in range(NC)]

    def terms_last(c):
        t2_r[c].wait_recv()
        t2_l[c].wait_recv()
        ts[c, 0] = (ts[c, 0].astype(f32) + trf[c, 0].astype(f32) + trf[c, 1].astype(f32)).astype(bf16)
        ig_cp[c].start()

    ad_cp = [lcopy(gown.at[c], ad_o.at[pl.ds(c * CH, CH)], out_s.at[NC + c]) for c in range(NC)]
    first_scale = 1.0 / (1.0 - beta_one**step_count)
    second_scale = 1.0 / (1.0 - beta_two**step_count)

    def adam(c):
        g_x[c].wait_recv()
        for cp in ad_loc[c]:
            cp.wait()

        @pl.loop(0, CH // 64)
        def _(i):
            rows = pl.ds(i * 64, 64)
            for a in range(2):
                cols = pl.ds(a * HC, HC)
                g = gown[c, rows, cols] + grecv[c, rows, cols].astype(f32)
                weight = adin[c % 2, 0, a, rows]
                moment = beta_one * adin[c % 2, 1, a, rows] + (1.0 - beta_one) * g
                second = beta_two * adin[c % 2, 2, a, rows] + (1.0 - beta_two) * g * g
                step = (moment * first_scale) / (jnp.sqrt(second * second_scale) + epsilon)
                gown[c, rows, cols] = weight - learn_rate * (step + decay_rate * weight)

        if c + 2 < NC:
            for cp in ad_loc[c + 2]:
                cp.start()
        ad_cp[c].start()

        @pl.loop(0, CH // 256)
        def _(i):
            rows = pl.ds(i * 256, 256)
            cols = pl.ds(pl.multiple_of(c * CH + i * 256, 256), 256)
            pan[:, cols] = dot_nt(st_ref[...], gown[c, rows].astype(bf16)).astype(bf16)

    send_h(0)
    for cp in dk_x:
        cp.start()
    send_h(1)
    convert_w(0)
    w_x[0].start()
    for c in (0, 1):
        for cp in ad_loc[c]:
            cp.start()
    for c in range(NC):
        forward_h(c)
        if c + 2 < NC:
            send_h(c + 2)
        if c + 1 < NC:
            convert_w(c + 1)
        if c == 0:
            for cp in dk_loc:
                cp.wait()
            for cp in dk_x:
                cp.wait_recv()
        grads(c)
        if c == 1:
            w_x[1].start()
    for c in range(2, NC):
        w_x[c].start()
    for c in range(NC):
        terms_first(c)
        produce(c)
        adam(c)
        terms_second(c)
        if c > 0:
            terms_last(c - 1)
    ko = []
    kx = []
    for s in range(4):
        for a in range(2):
            o = (keys_o, vals_o)[a].at[sl[s], z]
            kx.append(rcopy(kst.at[1, s, :, pl.ds(a * HC, HC)], o, ks_s.at[s, a], kr_s.at[s, a], pair))
            ko.append(lcopy(kst.at[0, s, :, pl.ds(a * HC, HC)], o, ko_s.at[s, a]))
    for cp in kx:
        cp.start()
    for cp in ko:
        cp.start()
    pan_cp = lcopy(pan, pan_o, out_s.at[2 * NC])
    pan_cp.start()
    terms_last(NC - 1)

    for cps in (h_r, h_l, f_r, f_l, dk_x, w_x, g_x, t1_r, t1_l, t2_r, t2_l, kx):
        for cp in cps:
            cp.wait_send()
    for cp in kx:
        cp.wait_recv()
    for cp in ko:
        cp.wait()
    for cp in ig_cp + ad_cp:
        cp.wait()
    pan_cp.wait()


def first_stage(h, wk, wv, mk, mv, sk, sv, gk, gv, start):
    dma = pltpu.SemaphoreType.DMA
    any_spec = pl.BlockSpec(memory_space=pl.ANY)
    shapes = (
        jax.ShapeDtypeStruct((4, 2, RB, HC), bf16),
        jax.ShapeDtypeStruct((4, 2, RB, HC), bf16),
        jax.ShapeDtypeStruct((RB, NC * CH), bf16),
        jax.ShapeDtypeStruct((NC * CH, 2 * HC), f32),
        jax.ShapeDtypeStruct((64, NC * CH), bf16),
    )
    scratch = [
        pltpu.VMEM((NC, 4, RB, CH), bf16),
        pltpu.VMEM((NC, 2, CH, 2 * HC), bf16),
        pltpu.VMEM((2, 4, RB, 2 * HC), bf16),
        pltpu.VMEM((NC, CH, 2 * HC), f32),
        pltpu.VMEM((NC, CH, 2 * HC), bf16),
        pltpu.VMEM((NC, CH, 2 * HC), bf16),
        pltpu.VMEM((2, 2, CH, HC), f32),
        pltpu.VMEM((2, 3, 2, CH, HC), f32),
        pltpu.VMEM((NC, 4, RB, CH), bf16),
        pltpu.VMEM((NC, 2, HR, CH), bf16),
        pltpu.VMEM((NC, 2, RB, CH), bf16),
        pltpu.VMEM((2, 4, RB, 2 * HC), f32),
        pltpu.VMEM((2, 4, RB, 2 * HC), bf16),
        pltpu.VMEM((64, NC * CH), bf16),
        dma((NC,)), dma((NC, 2)), dma((NC, 2)), dma((NC, 2)), dma((NC, 2)),
        dma((4, 2)), dma((4, 2)), dma((4, 2)), dma((2, 2)), dma((NC,)), dma((NC,)),
        dma((NC,)), dma((NC,)), dma((2, 3, 2)),
        dma((NC, 2)), dma((NC, 2)), dma((NC, 2)), dma((NC, 2)),
        dma((4, 2)), dma((4, 2)), dma((4, 2)), dma((2 * NC + 1,)),
    ]
    return pl.pallas_call(
        first_kernel,
        out_shape=shapes,
        in_specs=[any_spec] * 9 + [pl.BlockSpec(memory_space=pltpu.VMEM)],
        out_specs=[any_spec] * 5,
        scratch_shapes=scratch,
        compiler_params=pltpu.CompilerParams(
            collective_id=0, has_side_effects=True, vmem_limit_bytes=60 << 20
        ),
        cost_estimate=pl.CostEstimate(flops=13_000_000_000, bytes_accessed=60_000_000, transcendentals=0),
        name="first_stage",
    )(h, wk, wv, mk, mv, sk, sv, gk, gv, start)


def orthonormal(panel):
    gram_matrix = jnp.einsum("mds,mdt->mst", panel, panel, precision=lax.Precision.HIGHEST)
    lower_factor = jnp.linalg.cholesky(gram_matrix)
    return lax.linalg.triangular_solve(
        lower_factor, panel, left_side=False, lower=True, transpose_a=True
    )


def body(hidden, w_key, w_value, moment_key, moment_value, second_key, second_value,
         grad_keys, grad_values, seed_panels, partner):
    seeds = jnp.transpose(seed_panels, (0, 2, 1)).astype(bf16)
    zero = jnp.zeros_like(seeds[0])
    start = jnp.concatenate(
        [jnp.concatenate([seeds[0], zero], 1), jnp.concatenate([zero, seeds[1]], 1)], 0
    )
    keys, values, input_grad, adapted, panel = first_stage(
        hidden, w_key, w_value, moment_key, moment_value, second_key, second_value,
        grad_keys.reshape(4, 2, RB, HC), grad_values.reshape(4, 2, RB, HC), start,
    )
    adapted = jnp.stack([adapted[:, :HC], adapted[:, HC:]])
    own_index = lax.axis_index("replica")
    partner_id = partner[own_index]

    def fetch(panels):
        piece = lax.all_gather(panels[None].astype(bf16), "replica", axis=0, tiled=True)
        chosen = (jnp.arange(piece.shape[0]) == partner_id).reshape(
            (piece.shape[0],) + (1,) * panels.ndim
        )
        return jnp.zeros_like(panels) + jnp.sum(jnp.where(chosen, piece, 0.0), axis=0)

    panel_own = lax.psum(panel, "tensor").astype(f32)
    panel_own = jnp.transpose(panel_own.reshape(2, 32, NC * CH), (0, 2, 1))
    panel_diff = panel_own - fetch(panel_own)
    basis_panel = orthonormal(panel_diff)
    side_panel = jnp.einsum("mdc,mds->mcs", adapted, basis_panel, precision=lax.Precision.HIGHEST)
    side_diff = side_panel + fetch(side_panel)
    renewed = adapted - 0.5 * jnp.einsum(
        "mds,mcs->mdc", basis_panel, side_diff, precision=lax.Precision.HIGHEST
    )
    return (
        keys.reshape(8 * RB, HC), values.reshape(8 * RB, HC), input_grad,
        renewed[0][None], renewed[1][None],
    )


def solution(mesh):
    return jax.shard_map(
        body,
        mesh=mesh,
        in_specs=(
            P(("replica", "tensor"), None),
            P("replica", None, "tensor"),
            P("replica", None, "tensor"),
            P("replica", None, "tensor"),
            P("replica", None, "tensor"),
            P("replica", None, "tensor"),
            P("replica", None, "tensor"),
            P("replica", "tensor"),
            P("replica", "tensor"),
            P(None, "tensor", None),
            P(),
        ),
        out_specs=(
            P("replica", "tensor"),
            P("replica", "tensor"),
            P(("replica", "tensor"), None),
            P("replica", None, "tensor"),
            P("replica", None, "tensor"),
        ),
        check_vma=False,
    )
```

```python
import functools
import jax
import jax.numpy as jnp
from jax import lax
from jax.experimental import pallas as pl
from jax.experimental.pallas import tpu as pltpu
from jax.sharding import PartitionSpec as P

MESH = pl.DeviceIdType.MESH
beta_one = 0.9
beta_two = 0.95
epsilon = 1e-08
learn_rate = 0.06
decay_rate = 0.1
step_count = 100.0

NC = 5
CH = 1024
RB = 192
HR = 96
HC = 128
bf16 = jnp.bfloat16
f32 = jnp.float32


def slots(x):
    return (x, lax.rem(x + 3, 4), lax.rem(x + 1, 4), lax.rem(x + 2, 4))


def dot_tn(a, b):
    return lax.dot_general(a, b, (((0,), (0,)), ((), ())), preferred_element_type=f32)


def dot_nt(a, b):
    return lax.dot_general(a, b, (((1,), (1,)), ((), ())), preferred_element_type=f32)


def dot_nn(a, b):
    return lax.dot_general(a, b, (((1,), (0,)), ((), ())), preferred_element_type=f32)


def round_kernel(
    h_ref, wk_ref, wv_ref, mk_ref, mv_ref, sk_ref, sv_ref, gk_ref, gv_ref, st_ref, partner_ref,
    keys_o, vals_o, ig_o, nk_o, nv_o,
    hz, wp, dk, gown, gsend, grecv, wcv, adin, ts, trh, trf, kacc, kst,
    pan, prcv, osl, reps0, reps1, reps2, reps3, reps4, dfull, gacc, sacc, sside, srep, xhi, xlo,
    lh_s, hs_s, hr_s, fs_s, fr_s, ldk_s, dks_s, dkr_s, lw_s, ws_s, wr_s, gs_s, gr_s,
    lad_s, t1s_s, t1r_s, t2s_s, t2r_s, ko_s, ks_s, kr_s, out_s,
    ps_s, pr_s, os_s, or_s, ds_s, dr_s, ss_s, sr_s,
):
    r = lax.axis_index("replica")
    t = lax.axis_index("tensor")
    x = t // 2
    z = lax.rem(t, 2)
    right = (r, lax.rem(x + 1, 4) * 2 + z)
    left = (r, lax.rem(x + 3, 4) * 2 + z)
    pair = (r, x * 2 + (1 - z))
    sl = slots(x)
    reps = (reps0, reps1, reps2, reps3, reps4)
    g_refs = (gk_ref, gv_ref)
    w_refs = (wk_ref, wv_ref)
    ad_refs = ((wk_ref, wv_ref), (mk_ref, mv_ref), (sk_ref, sv_ref))

    def rcopy(src, dst, ssem, rsem, dev):
        return pltpu.make_async_remote_copy(
            src_ref=src, dst_ref=dst, send_sem=ssem, recv_sem=rsem,
            device_id=dev, device_id_type=MESH,
        )

    def lcopy(src, dst, sem):
        return pltpu.make_async_copy(src, dst, sem)

    dk_loc = [
        lcopy(g_refs[a].at[sl[s], z], dk.at[0, s, :, pl.ds(a * HC, HC)], ldk_s.at[s, a])
        for s in range(4) for a in range(2)
    ]
    h_loc = [lcopy(h_ref.at[:, pl.ds(c * CH, CH)], hz.at[c, 0], lh_s.at[c]) for c in range(NC)]
    w_loc = [
        [lcopy(w_refs[a].at[0, pl.ds(c * CH, CH)], wcv.at[c % 2, a], lw_s.at[c % 2, a]) for a in range(2)]
        for c in range(NC)
    ]
    ad_loc = [
        [
            lcopy(ad_refs[k][a].at[0, pl.ds(c * CH, CH)], adin.at[c % 2, k, a], lad_s.at[c % 2, k, a])
            for k in range(3) for a in range(2)
        ]
        for c in range(NC)
    ]
    for c in (0, 1):
        for cp in w_loc[c]:
            cp.start()
    for cp in dk_loc:
        cp.start()
    for cp in h_loc:
        cp.start()

    barrier = pltpu.get_barrier_semaphore()
    for k in range(1, 8):
        pl.semaphore_signal(barrier, inc=1, device_id=(r, lax.rem(t + k, 8)), device_id_type=MESH)
    for k in range(1, 16):
        pl.semaphore_signal(barrier, inc=1, device_id=(lax.rem(r + k, 16), t), device_id_type=MESH)
    pl.semaphore_wait(barrier, 22)

    h_r = [rcopy(h_ref.at[:, pl.ds(c * CH, CH)], hz.at[c, 1], hs_s.at[c, 0], hr_s.at[c, 0], right) for c in range(NC)]
    h_l = [rcopy(h_ref.at[:, pl.ds(c * CH, CH)], hz.at[c, 2], hs_s.at[c, 1], hr_s.at[c, 1], left) for c in range(NC)]
    f_r = [rcopy(hz.at[c, 1, pl.ds(0, HR)], hz.at[c, 3, pl.ds(0, HR)], fs_s.at[c, 0], fr_s.at[c, 0], right) for c in range(NC)]
    f_l = [rcopy(hz.at[c, 2, pl.ds(HR, HR)], hz.at[c, 3, pl.ds(HR, HR)], fs_s.at[c, 1], fr_s.at[c, 1], left) for c in range(NC)]
    dk_x = [
        rcopy(g_refs[a].at[sl[s], 1 - z], dk.at[1, s, :, pl.ds(a * HC, HC)], dks_s.at[s, a], dkr_s.at[s, a], pair)
        for s in range(4) for a in range(2)
    ]
    w_x = [rcopy(wp.at[c, 0], wp.at[c, 1], ws_s.at[c], wr_s.at[c], pair) for c in range(NC)]
    g_x = [rcopy(gsend.at[c], grecv.at[c], gs_s.at[c], gr_s.at[c], pair) for c in range(NC)]
    t1_r = [rcopy(ts.at[c, 3, pl.ds(0, HR)], trh.at[c, 0], t1s_s.at[c, 0], t1r_s.at[c, 0], right) for c in range(NC)]
    t1_l = [rcopy(ts.at[c, 3, pl.ds(HR, HR)], trh.at[c, 1], t1s_s.at[c, 1], t1r_s.at[c, 1], left) for c in range(NC)]
    t2_r = [rcopy(ts.at[c, 2], trf.at[c, 0], t2s_s.at[c, 0], t2r_s.at[c, 0], right) for c in range(NC)]
    t2_l = [rcopy(ts.at[c, 1], trf.at[c, 1], t2s_s.at[c, 1], t2r_s.at[c, 1], left) for c in range(NC)]

    def send_h(c):
        h_r[c].start()
        h_l[c].start()

    def convert_w(c):
        for cp in w_loc[c]:
            cp.wait()

        @pl.loop(0, CH // 256)
        def _(i):
            rows = pl.ds(i * 256, 256)
            for a in range(2):
                wp[c, 0, rows, pl.ds(a * HC, HC)] = wcv[c % 2, a, rows].astype(bf16)

        if c + 2 < NC:
            for cp in w_loc[c + 2]:
                cp.start()

    def forward_h(c):
        h_r[c].wait_recv()
        f_r[c].start()
        h_l[c].wait_recv()
        f_l[c].start()

    def grads(c):
        h_loc[c].wait()
        f_r[c].wait_recv()
        f_l[c].wait_recv()

        @pl.loop(0, CH // 256)
        def _(i):
            cols = pl.ds(pl.multiple_of(i * 256, 256), 256)
            rows = pl.ds(i * 256, 256)
            lhs = hz[c, :, :, cols].reshape(4 * RB, 256)
            gsend[c, rows] = dot_tn(lhs, dk[1].reshape(4 * RB, 2 * HC)).astype(bf16)
            gown[c, rows] = dot_tn(lhs, dk[0].reshape(4 * RB, 2 * HC))

    def produce(c):
        for s in range(4):
            for p in range(2):
                add = dot_nn(hz[c, s], wp[c, p])
                if c == 0:
                    kacc[p, s] = add
                elif c < NC - 1:
                    kacc[p, s] = kacc[p, s] + add
                else:
                    kst[p, s] = (kacc[p, s] + add).astype(bf16)

    def term(c, s):
        @pl.loop(0, CH // 256)
        def _(i):
            cols = pl.ds(pl.multiple_of(i * 256, 256), 256)
            rows = pl.ds(i * 256, 256)
            ts[c, s, :, cols] = (
                dot_nt(dk[0, s], wp[c, 0, rows]) + dot_nt(dk[1, s], wp[c, 1, rows])
            ).astype(bf16)

    def terms_first(c):
        w_x[c].wait_recv()
        term(c, 3)
        t1_r[c].start()
        t1_l[c].start()
        term(c, 2)
        term(c, 1)
        term(c, 0)

    def terms_second(c):
        t1_r[c].wait_recv()
        ts[c, 2, pl.ds(0, HR)] = (ts[c, 2, pl.ds(0, HR)].astype(f32) + trh[c, 0].astype(f32)).astype(bf16)
        t2_r[c].start()
        t1_l[c].wait_recv()
        ts[c, 1, pl.ds(HR, HR)] = (ts[c, 1, pl.ds(HR, HR)].astype(f32) + trh[c, 1].astype(f32)).astype(bf16)
        t2_l[c].start()

    ig_cp = [lcopy(ts.at[c, 0], ig_o.at[:, pl.ds(c * CH, CH)], out_s.at[c]) for c in range(NC)]

    def terms_last(c):
        t2_r[c].wait_recv()
        t2_l[c].wait_recv()
        ts[c, 0] = (ts[c, 0].astype(f32) + trf[c, 0].astype(f32) + trf[c, 1].astype(f32)).astype(bf16)
        ig_cp[c].start()

    first_scale = 1.0 / (1.0 - beta_one**step_count)
    second_scale = 1.0 / (1.0 - beta_two**step_count)

    def adam(c):
        g_x[c].wait()
        for cp in ad_loc[c]:
            cp.wait()

        @pl.loop(0, CH // 64)
        def _(i):
            rows = pl.ds(i * 64, 64)
            for a in range(2):
                cols = pl.ds(a * HC, HC)
                g = gown[c, rows, cols] + grecv[c, rows, cols].astype(f32)
                weight = adin[c % 2, 0, a, rows]
                moment = beta_one * adin[c % 2, 1, a, rows] + (1.0 - beta_one) * g
                second = beta_two * adin[c % 2, 2, a, rows] + (1.0 - beta_two) * g * g
                step = (moment * first_scale) / (jnp.sqrt(second * second_scale) + epsilon)
                new = weight - learn_rate * (step + decay_rate * weight)
                gown[c, rows, cols] = new
                gsend[c, rows, cols] = new.astype(bf16)

        if c + 2 < NC:
            for cp in ad_loc[c + 2]:
                cp.start()

        @pl.loop(0, CH // 256)
        def _(i):
            rows = pl.ds(i * 256, 256)
            tile = dot_nt(st_ref[...], gsend[c, rows]).astype(bf16)
            pan[c, 2 * i] = tile[:, :HC]
            pan[c, 2 * i + 1] = tile[:, HC:]

        @pl.loop(1, 8)
        def _(k):
            pan_copy(c, k).start()

    def pan_copy(c, k):
        j = lax.rem(t + k, 8)
        return rcopy(pan.at[c, j], prcv.at[c, k], ps_s.at[c, k], pr_s.at[c, k], (r, j))

    def slab_copy(c, k):
        return rcopy(osl.at[c], reps[c].at[k], os_s.at[c, k], or_s.at[c, k], (lax.rem(r + k, 16), t))

    mine = pl.ds(pl.multiple_of(t * HC, HC), HC)

    def diff_copy(c, k):
        part = dfull.at[c, :, mine]
        return rcopy(part, part, ds_s.at[c, k], dr_s.at[c, k], (r, lax.rem(t + k, 8)))

    def side_copy(k):
        return rcopy(sside, srep.at[k], ss_s.at[k], sr_s.at[k], (lax.rem(r + k, 16), t))

    away = lax.rem(r - partner_ref[r] + 16, 16)

    def slab(c):
        for k in range(1, 8):
            pan_copy(c, k).wait_recv()
        total = pan[c, t].astype(f32)
        for k in range(1, 8):
            total = total + prcv[c, k].astype(f32)
        osl[c] = total.astype(bf16)

        @pl.loop(1, 16)
        def _(k):
            slab_copy(c, k).start()

    def diff(c):
        @pl.loop(1, 16)
        def _(k):
            slab_copy(c, k).wait_recv()

        dfull[c, :, mine] = (osl[c].astype(f32) - reps[c][away].astype(f32)).astype(bf16)

        @pl.loop(1, 8)
        def _(k):
            diff_copy(c, k).start()

    def gram_side(c):
        @pl.loop(1, 8)
        def _(k):
            diff_recv(c, k).wait_recv()

        d = dfull[c]
        gram = dot_nt(d, d)
        side = dot_nn(d, gsend[c])
        if c == 0:
            gacc[...] = gram
            sacc[...] = side
        else:
            gacc[...] = gacc[...] + gram
            sacc[...] = sacc[...] + side

    def diff_recv(c, k):
        part = dfull.at[c, :, pl.ds(pl.multiple_of(lax.rem(t + 8 - k, 8) * HC, HC), HC)]
        return rcopy(part, part, ds_s.at[c, k], dr_s.at[c, k], (r, lax.rem(t + k, 8)))

    def side_send():
        sside[pl.ds(0, 32)] = sacc[pl.ds(0, 32), pl.ds(0, HC)].astype(bf16)
        sside[pl.ds(32, 32)] = sacc[pl.ds(32, 32), pl.ds(HC, HC)].astype(bf16)

        @pl.loop(1, 16)
        def _(k):
            side_copy(k).start()

    def inverses(mats):
        row_at = lax.broadcasted_iota(jnp.int32, (32, 32), 0)
        col_at = lax.broadcasted_iota(jnp.int32, (32, 32), 1)
        for k in range(32):
            step = []
            for m in mats:
                inv = 1.0 / m[k : k + 1, k : k + 1]
                row = jnp.where(col_at[:1] == k, inv, m[k : k + 1] * inv)
                col = m[:, k : k + 1]
                step.append(jnp.where(row_at == k, row, jnp.where(col_at == k, 0.0, m) - col * row))
            mats = step
        return mats

    def solve():
        gram = gacc[...]
        inv = inverses([gram[:32, :32], gram[32:, 32:]])

        @pl.loop(1, 16)
        def _(k):
            side_copy(k).wait_recv()

        other = srep[away].astype(f32)
        xhi[...] = jnp.zeros_like(xhi)
        xlo[...] = jnp.zeros_like(xlo)
        for a in range(2):
            rows, cols = pl.ds(a * 32, 32), pl.ds(a * HC, HC)
            total = sacc[rows, cols] + other[a * 32 : a * 32 + 32]
            x_a = 0.5 * lax.dot_general(
                inv[a], total, (((1,), (0,)), ((), ())),
                precision=lax.Precision.HIGHEST, preferred_element_type=f32,
            )
            high = x_a.astype(bf16)
            xhi[rows, cols] = high
            xlo[rows, cols] = (x_a - high.astype(f32)).astype(bf16)

    new_cp = [
        lcopy(gown.at[c, :, pl.ds(a * HC, HC)], (nk_o, nv_o)[a].at[0, pl.ds(c * CH, CH)], out_s.at[NC + 2 * c + a])
        for c in range(NC) for a in range(2)
    ]

    def renew(c):
        @pl.loop(0, CH // 256)
        def _(i):
            cols = pl.ds(pl.multiple_of(i * 256, 256), 256)
            rows = pl.ds(i * 256, 256)
            lhs = dfull[c, :, cols]
            gown[c, rows] = gown[c, rows] - (dot_tn(lhs, xhi[...]) + dot_tn(lhs, xlo[...]))

        new_cp[2 * c].start()
        new_cp[2 * c + 1].start()

    send_h(0)
    for cp in dk_x:
        cp.start()
    send_h(1)
    convert_w(0)
    w_x[0].start()
    for c in (0, 1):
        for cp in ad_loc[c]:
            cp.start()
    def arrive(c):
        forward_h(c)
        if c + 2 < NC:
            send_h(c + 2)
        if c + 1 < NC:
            convert_w(c + 1)
        if c == 0:
            for cp in dk_loc:
                cp.wait()
            for cp in dk_x:
                cp.wait_recv()
        grads(c)

    ko = []
    kx = []
    for s in range(4):
        for a in range(2):
            o = (keys_o, vals_o)[a].at[sl[s], z]
            kx.append(rcopy(kst.at[1, s, :, pl.ds(a * HC, HC)], o, ks_s.at[s, a], kr_s.at[s, a], pair))
            ko.append(lcopy(kst.at[0, s, :, pl.ds(a * HC, HC)], o, ko_s.at[s, a]))

    def keys_send(first, last):
        for cp in kx[first:last] + ko[first:last]:
            cp.start()

    arrive(0)
    g_x[0].start()
    w_x[1].start()
    arrive(1)
    g_x[1].start()
    adam(0)
    w_x[2].start()
    arrive(2)
    g_x[2].start()
    arrive(3)
    adam(1)
    slab(0)
    w_x[3].start()
    g_x[3].start()
    arrive(4)
    terms_first(0)
    produce(0)
    adam(2)
    w_x[4].start()
    g_x[4].start()
    terms_first(1)
    terms_second(0)
    produce(1)
    slab(1)
    diff(0)
    terms_first(2)
    terms_second(1)
    terms_last(0)
    produce(2)
    adam(3)
    slab(2)
    diff(1)
    gram_side(0)
    terms_first(3)
    terms_second(2)
    terms_last(1)
    produce(3)
    terms_first(4)
    terms_second(3)
    terms_last(2)
    produce(4)
    adam(4)
    gram_side(1)
    slab(3)
    diff(2)
    terms_second(4)
    keys_send(0, 2)
    slab(4)
    diff(3)
    gram_side(2)
    keys_send(2, 4)
    terms_last(3)
    diff(4)
    gram_side(3)
    gram_side(4)
    side_send()
    keys_send(4, 8)
    terms_last(4)
    solve()
    for c in range(NC):
        renew(c)

    for cps in (h_r, h_l, f_r, f_l, dk_x, w_x, t1_r, t1_l, t2_r, t2_l, kx):
        for cp in cps:
            cp.wait_send()
    for cp in kx:
        cp.wait_recv()
    for cp in ko:
        cp.wait()
    for cp in ig_cp + new_cp:
        cp.wait()

    @pl.loop(1, 8)
    def _(k):
        for c in range(NC):
            pan_copy(c, k).wait_send()
            diff_copy(c, k).wait_send()

    @pl.loop(1, 16)
    def _(k):
        for c in range(NC):
            slab_copy(c, k).wait_send()
        side_copy(k).wait_send()


def gossip_round(h, wk, wv, mk, mv, sk, sv, gk, gv, start, partner):
    dma = pltpu.SemaphoreType.DMA
    any_spec = pl.BlockSpec(memory_space=pl.ANY)
    shapes = (
        jax.ShapeDtypeStruct((4, 2, RB, HC), bf16),
        jax.ShapeDtypeStruct((4, 2, RB, HC), bf16),
        jax.ShapeDtypeStruct((RB, NC * CH), bf16),
        jax.ShapeDtypeStruct((1, NC * CH, HC), f32),
        jax.ShapeDtypeStruct((1, NC * CH, HC), f32),
    )
    scratch = [
        pltpu.VMEM((NC, 4, RB, CH), bf16),
        pltpu.VMEM((NC, 2, CH, 2 * HC), bf16),
        pltpu.VMEM((2, 4, RB, 2 * HC), bf16),
        pltpu.VMEM((NC, CH, 2 * HC), f32),
        pltpu.VMEM((NC, CH, 2 * HC), bf16),
        pltpu.VMEM((NC, CH, 2 * HC), bf16),
        pltpu.VMEM((2, 2, CH, HC), f32),
        pltpu.VMEM((2, 3, 2, CH, HC), f32),
        pltpu.VMEM((NC, 4, RB, CH), bf16),
        pltpu.VMEM((NC, 2, HR, CH), bf16),
        pltpu.VMEM((NC, 2, RB, CH), bf16),
        pltpu.VMEM((2, 4, RB, 2 * HC), f32),
        pltpu.VMEM((2, 4, RB, 2 * HC), bf16),
        pltpu.VMEM((NC, 8, 64, HC), bf16),
        pltpu.VMEM((NC, 8, 64, HC), bf16),
        pltpu.VMEM((NC, 64, HC), bf16),
        *[pltpu.VMEM((16, 64, HC), bf16) for _ in range(NC)],
        pltpu.VMEM((NC, 64, CH), bf16),
        pltpu.VMEM((64, 64), f32),
        pltpu.VMEM((64, 2 * HC), f32),
        pltpu.VMEM((64, HC), bf16),
        pltpu.VMEM((16, 64, HC), bf16),
        pltpu.VMEM((64, 2 * HC), bf16),
        pltpu.VMEM((64, 2 * HC), bf16),
        dma((NC,)), dma((NC, 2)), dma((NC, 2)), dma((NC, 2)), dma((NC, 2)),
        dma((4, 2)), dma((4, 2)), dma((4, 2)), dma((2, 2)), dma((NC,)), dma((NC,)),
        dma((NC,)), dma((NC,)), dma((2, 3, 2)),
        dma((NC, 2)), dma((NC, 2)), dma((NC, 2)), dma((NC, 2)),
        dma((4, 2)), dma((4, 2)), dma((4, 2)), dma((3 * NC,)),
        dma((NC, 8)), dma((NC, 8)), dma((NC, 16)), dma((NC, 16)),
        dma((NC, 8)), dma((NC, 8)), dma((16,)), dma((16,)),
    ]
    return pl.pallas_call(
        round_kernel,
        out_shape=shapes,
        in_specs=[any_spec] * 9
        + [pl.BlockSpec(memory_space=pltpu.VMEM), pl.BlockSpec(memory_space=pltpu.SMEM)],
        out_specs=[any_spec] * 5,
        scratch_shapes=scratch,
        compiler_params=pltpu.CompilerParams(
            collective_id=0, has_side_effects=True, vmem_limit_bytes=60 << 20
        ),
        cost_estimate=pl.CostEstimate(flops=13_000_000_000, bytes_accessed=60_000_000, transcendentals=0),
        name="gossip_round",
    )(h, wk, wv, mk, mv, sk, sv, gk, gv, start, partner)


def body(hidden, w_key, w_value, moment_key, moment_value, second_key, second_value,
         grad_keys, grad_values, seed_panels, partner):
    seeds = jnp.transpose(seed_panels, (0, 2, 1)).astype(bf16)
    zero = jnp.zeros_like(seeds[0])
    start = jnp.concatenate(
        [jnp.concatenate([seeds[0], zero], 1), jnp.concatenate([zero, seeds[1]], 1)], 0
    )
    keys, values, input_grad, new_key, new_value = gossip_round(
        hidden, w_key, w_value, moment_key, moment_value, second_key, second_value,
        grad_keys.reshape(4, 2, RB, HC), grad_values.reshape(4, 2, RB, HC), start, partner,
    )
    return keys.reshape(8 * RB, HC), values.reshape(8 * RB, HC), input_grad, new_key, new_value


def solution(mesh):
    return jax.shard_map(
        body,
        mesh=mesh,
        in_specs=(
            P(("replica", "tensor"), None),
            P("replica", None, "tensor"),
            P("replica", None, "tensor"),
            P("replica", None, "tensor"),
            P("replica", None, "tensor"),
            P("replica", None, "tensor"),
            P("replica", None, "tensor"),
            P("replica", "tensor"),
            P("replica", "tensor"),
            P(None, "tensor", None),
            P(),
        ),
        out_specs=(
            P("replica", "tensor"),
            P("replica", "tensor"),
            P(("replica", "tensor"), None),
            P("replica", None, "tensor"),
            P("replica", None, "tensor"),
        ),
        check_vma=False,
    )
```

```python
import functools
import jax
import jax.numpy as jnp
from jax import lax
from jax.experimental import pallas as pl
from jax.experimental.pallas import tpu as pltpu
from jax.sharding import PartitionSpec as P

MESH = pl.DeviceIdType.MESH
beta_one = 0.9
beta_two = 0.95
epsilon = 1e-08
learn_rate = 0.06
decay_rate = 0.1
step_count = 100.0

NC = 5
CH = 1024
RB = 192
HR = 96
HC = 128
bf16 = jnp.bfloat16
f32 = jnp.float32


def slots(x):
    return (x, lax.rem(x + 3, 4), lax.rem(x + 1, 4), lax.rem(x + 2, 4))


def dot_tn(a, b):
    return lax.dot_general(a, b, (((0,), (0,)), ((), ())), preferred_element_type=f32)


def dot_nt(a, b):
    return lax.dot_general(a, b, (((1,), (1,)), ((), ())), preferred_element_type=f32)


def dot_nn(a, b):
    return lax.dot_general(a, b, (((1,), (0,)), ((), ())), preferred_element_type=f32)


def round_kernel(
    h_ref, wk_ref, wv_ref, mk_ref, mv_ref, sk_ref, sv_ref, gk_ref, gv_ref, st_ref, partner_ref,
    keys_o, vals_o, ig_o, nk_o, nv_o,
    hz, wp, dk, gown, gsend, grecv, wcv, adin, ts, trh, trf, kacc, kst,
    pan, prx, psend, prz, quad0, quad1, quad2, ysend0, ysend1, ysend2, yall0, yall1, yall2,
    dfull, gacc, sacc, xhi, xlo,
    lh_s, hs_s, hr_s, fs_s, fr_s, ldk_s, dks_s, dkr_s, lw_s, ws_s, wr_s, gs_s, gr_s,
    lad_s, t1s_s, t1r_s, t2s_s, t2r_s, ko_s, ks_s, kr_s, out_s,
    px_s, px_r, pz_s, pz_r, qs_s, qr_s, ys_s, yr_s, dz_s, dz_r, dx_s, dx_r,
):
    r = lax.axis_index("replica")
    t = lax.axis_index("tensor")
    x = t // 2
    z = lax.rem(t, 2)
    right = (r, lax.rem(x + 1, 4) * 2 + z)
    left = (r, lax.rem(x + 3, 4) * 2 + z)
    pair = (r, x * 2 + (1 - z))
    sl = slots(x)
    quads, ysends, yalls = (quad0, quad1, quad2), (ysend0, ysend1, ysend2), (yall0, yall1, yall2)
    y = r // 4
    zl = lax.rem(r // 2, 2)
    core = lax.rem(r, 2)
    near = (
        (y * 4 + zl * 2 + 1 - core, t),
        (y * 4 + (1 - zl) * 2 + core, t),
        (y * 4 + (1 - zl) * 2 + 1 - core, t),
    )
    g_refs = (gk_ref, gv_ref)
    w_refs = (wk_ref, wv_ref)
    ad_refs = ((wk_ref, wv_ref), (mk_ref, mv_ref), (sk_ref, sv_ref))

    def rcopy(src, dst, ssem, rsem, dev):
        return pltpu.make_async_remote_copy(
            src_ref=src, dst_ref=dst, send_sem=ssem, recv_sem=rsem,
            device_id=dev, device_id_type=MESH,
        )

    def lcopy(src, dst, sem):
        return pltpu.make_async_copy(src, dst, sem)

    dk_loc = [
        lcopy(g_refs[a].at[sl[s], z], dk.at[0, s, :, pl.ds(a * HC, HC)], ldk_s.at[s, a])
        for s in range(4) for a in range(2)
    ]
    h_loc = [lcopy(h_ref.at[:, pl.ds(c * CH, CH)], hz.at[c, 0], lh_s.at[c]) for c in range(NC)]
    w_loc = [
        [lcopy(w_refs[a].at[0, pl.ds(c * CH, CH)], wcv.at[c % 2, a], lw_s.at[c % 2, a]) for a in range(2)]
        for c in range(NC)
    ]
    ad_loc = [
        [
            lcopy(ad_refs[k][a].at[0, pl.ds(c * CH, CH)], adin.at[c % 2, k, a], lad_s.at[c % 2, k, a])
            for k in range(3) for a in range(2)
        ]
        for c in range(NC)
    ]
    for c in (0, 1):
        for cp in w_loc[c]:
            cp.start()
    for cp in dk_loc:
        cp.start()
    for cp in h_loc:
        cp.start()

    barrier = pltpu.get_barrier_semaphore()
    peers = [pair, *near]
    for k in range(1, 4):
        peers.append((r, lax.rem(x + k, 4) * 2 + z))
        peers.append((lax.rem(r + 4 * k, 16), t))
    for dev in peers:
        pl.semaphore_signal(barrier, inc=1, device_id=dev, device_id_type=MESH)
    pl.semaphore_wait(barrier, len(peers))

    h_r = [rcopy(h_ref.at[:, pl.ds(c * CH, CH)], hz.at[c, 1], hs_s.at[c, 0], hr_s.at[c, 0], right) for c in range(NC)]
    h_l = [rcopy(h_ref.at[:, pl.ds(c * CH, CH)], hz.at[c, 2], hs_s.at[c, 1], hr_s.at[c, 1], left) for c in range(NC)]
    f_r = [rcopy(hz.at[c, 1, pl.ds(0, HR)], hz.at[c, 3, pl.ds(0, HR)], fs_s.at[c, 0], fr_s.at[c, 0], right) for c in range(NC)]
    f_l = [rcopy(hz.at[c, 2, pl.ds(HR, HR)], hz.at[c, 3, pl.ds(HR, HR)], fs_s.at[c, 1], fr_s.at[c, 1], left) for c in range(NC)]
    dk_x = [
        rcopy(g_refs[a].at[sl[s], 1 - z], dk.at[1, s, :, pl.ds(a * HC, HC)], dks_s.at[s, a], dkr_s.at[s, a], pair)
        for s in range(4) for a in range(2)
    ]
    w_x = [rcopy(wp.at[c, 0], wp.at[c, 1], ws_s.at[c], wr_s.at[c], pair) for c in range(NC)]
    g_x = [rcopy(gsend.at[c], grecv.at[c], gs_s.at[c], gr_s.at[c], pair) for c in range(NC)]
    t1_r = [rcopy(ts.at[c, 3, pl.ds(0, HR)], trh.at[c, 0], t1s_s.at[c, 0], t1r_s.at[c, 0], right) for c in range(NC)]
    t1_l = [rcopy(ts.at[c, 3, pl.ds(HR, HR)], trh.at[c, 1], t1s_s.at[c, 1], t1r_s.at[c, 1], left) for c in range(NC)]
    t2_r = [rcopy(ts.at[c, 2], trf.at[c, 0], t2s_s.at[c, 0], t2r_s.at[c, 0], right) for c in range(NC)]
    t2_l = [rcopy(ts.at[c, 1], trf.at[c, 1], t2s_s.at[c, 1], t2r_s.at[c, 1], left) for c in range(NC)]

    def send_h(c):
        h_r[c].start()
        h_l[c].start()

    def convert_w(c):
        for cp in w_loc[c]:
            cp.wait()

        @pl.loop(0, CH // 256)
        def _(i):
            rows = pl.ds(i * 256, 256)
            for a in range(2):
                wp[c, 0, rows, pl.ds(a * HC, HC)] = wcv[c % 2, a, rows].astype(bf16)

        if c + 2 < NC:
            for cp in w_loc[c + 2]:
                cp.start()

    def forward_h(c):
        h_r[c].wait_recv()
        f_r[c].start()
        h_l[c].wait_recv()
        f_l[c].start()

    def grads(c):
        h_loc[c].wait()
        f_r[c].wait_recv()
        f_l[c].wait_recv()

        @pl.loop(0, CH // 256)
        def _(i):
            cols = pl.ds(pl.multiple_of(i * 256, 256), 256)
            rows = pl.ds(i * 256, 256)
            lhs = hz[c, :, :, cols].reshape(4 * RB, 256).T
            gsend[c, rows] = dot_nn(lhs, dk[1].reshape(4 * RB, 2 * HC)).astype(bf16)
            gown[c, rows] = dot_nn(lhs, dk[0].reshape(4 * RB, 2 * HC))

    def produce(c):
        for p in range(2):
            add = dot_nn(hz[c].reshape(4 * RB, CH), wp[c, p]).reshape(4, RB, 2 * HC)
            if c == 0:
                kacc[p] = add
            elif c < NC - 1:
                kacc[p] = kacc[p] + add
            else:
                kst[p] = (kacc[p] + add).astype(bf16)

    def terms_first(c):
        w_x[c].wait_recv()

        @pl.loop(0, CH // 256)
        def _(i):
            cols = pl.ds(pl.multiple_of(i * 256, 256), 256)
            rows = pl.ds(i * 256, 256)
            total = dot_nt(dk[0].reshape(4 * RB, 2 * HC), wp[c, 0, rows])
            total = total + dot_nt(dk[1].reshape(4 * RB, 2 * HC), wp[c, 1, rows])
            ts[c, :, :, cols] = total.astype(bf16).reshape(4, RB, 256)

        t1_r[c].start()
        t1_l[c].start()

    def terms_second(c):
        t1_r[c].wait_recv()
        ts[c, 2, pl.ds(0, HR)] = (ts[c, 2, pl.ds(0, HR)].astype(f32) + trh[c, 0].astype(f32)).astype(bf16)
        t2_r[c].start()
        t1_l[c].wait_recv()
        ts[c, 1, pl.ds(HR, HR)] = (ts[c, 1, pl.ds(HR, HR)].astype(f32) + trh[c, 1].astype(f32)).astype(bf16)
        t2_l[c].start()

    ig_cp = [lcopy(ts.at[c, 0], ig_o.at[:, pl.ds(c * CH, CH)], out_s.at[c]) for c in range(NC)]

    def terms_last(c):
        t2_r[c].wait_recv()
        t2_l[c].wait_recv()
        ts[c, 0] = (ts[c, 0].astype(f32) + trf[c, 0].astype(f32) + trf[c, 1].astype(f32)).astype(bf16)
        ig_cp[c].start()

    first_scale = 1.0 / (1.0 - beta_one**step_count)
    second_scale = 1.0 / (1.0 - beta_two**step_count)

    def adam(c):
        g_x[c].wait()
        for cp in ad_loc[c]:
            cp.wait()

        @pl.loop(0, CH // 64)
        def _(i):
            rows = pl.ds(i * 64, 64)
            for a in range(2):
                cols = pl.ds(a * HC, HC)
                g = gown[c, rows, cols] + grecv[c, rows, cols].astype(f32)
                weight = adin[c % 2, 0, a, rows]
                moment = beta_one * adin[c % 2, 1, a, rows] + (1.0 - beta_one) * g
                second = beta_two * adin[c % 2, 2, a, rows] + (1.0 - beta_two) * g * g
                step = (moment * first_scale) / (jnp.sqrt(second * second_scale) + epsilon)
                new = weight - learn_rate * (step + decay_rate * weight)
                gown[c, rows, cols] = new
                gsend[c, rows, cols] = new.astype(bf16)

        if c + 2 < NC:
            for cp in ad_loc[c + 2]:
                cp.start()

        @pl.loop(0, CH // 256)
        def _(i):
            rows = pl.ds(i * 256, 256)
            tile = dot_nt(st_ref[...], gsend[c, rows]).astype(bf16)
            pan[c, 2 * i] = tile[:, :HC]
            pan[c, 2 * i + 1] = tile[:, HC:]

    groups = ((0, 3), (3, 2))

    def chunks(g):
        return pl.ds(groups[g][0], groups[g][1])

    def pan_x(g):
        return [
            rcopy(
                pan.at[chunks(g), pl.ds(lax.rem(x + k, 4) * 2, 2)], prx.at[chunks(g), k - 1],
                px_s.at[g, k], px_r.at[g, k], (r, lax.rem(x + k, 4) * 2 + z),
            )
            for k in range(1, 4)
        ]

    def pan_z(g):
        return [rcopy(psend.at[chunks(g)], prz.at[chunks(g)], pz_s.at[g], pz_r.at[g], pair)]

    def quad_x(g):
        part = quads[g].at[:, zl, core]
        return [rcopy(part, part, qs_s.at[g, k], qr_s.at[g, k], near[k]) for k in range(3)]

    def quad_r(g):
        from_at = ((zl, 1 - core), (1 - zl, core), (1 - zl, 1 - core))
        return [
            rcopy(quads[g].at[:, a, b], quads[g].at[:, a, b], qs_s.at[g, k], qr_s.at[g, k], near[k])
            for k, (a, b) in enumerate(from_at)
        ]

    def y_x(g):
        return [
            rcopy(
                ysends[g].at[k - 1], yalls[g].at[k], ys_s.at[g, k], yr_s.at[g, k],
                (lax.rem(r + 4 * k, 16), t),
            )
            for k in range(1, 4)
        ]

    mine = pl.ds(pl.multiple_of(t * HC, HC), HC)

    def both(at):
        return pl.ds(pl.multiple_of(at * 2 * HC, 2 * HC), 2 * HC)

    def diff_z(g):
        part = dfull.at[chunks(g), :, mine]
        return [rcopy(part, part, dz_s.at[g], dz_r.at[g], pair)]

    def diff_zr(g):
        part = dfull.at[chunks(g), :, pl.ds(pl.multiple_of((x * 2 + 1 - z) * HC, HC), HC)]
        return [rcopy(part, part, dz_s.at[g], dz_r.at[g], pair)]

    def diff_x(g):
        part = dfull.at[chunks(g), :, both(x)]
        return [
            rcopy(part, part, dx_s.at[g, k], dx_r.at[g, k], (r, lax.rem(x + k, 4) * 2 + z))
            for k in range(1, 4)
        ]

    def diff_xr(g):
        out = []
        for k in range(1, 4):
            part = dfull.at[chunks(g), :, both(lax.rem(x + 4 - k, 4))]
            out.append(rcopy(part, part, dx_s.at[g, k], dx_r.at[g, k], (r, lax.rem(x + k, 4) * 2 + z)))
        return out

    def start(cps):
        for cp in cps:
            cp.start()

    def arrived(cps):
        for cp in cps:
            cp.wait_recv()

    def panel_x(g):
        start(pan_x(g))

    def panel_z(g):
        arrived(pan_x(g))
        first, count = groups[g]
        for c in range(first, first + count):
            total = pan[c, x * 2 + 1 - z].astype(f32)
            for k in range(3):
                total = total + prx[c, k, 1 - z].astype(f32)
            psend[c] = total.astype(bf16)
        start(pan_z(g))

    def slab_near(g):
        arrived(pan_z(g))
        first, count = groups[g]
        for c in range(first, first + count):
            total = pan[c, t].astype(f32) + prz[c].astype(f32)
            for k in range(3):
                total = total + prx[c, k, z].astype(f32)
            quads[g][c - first, zl, core] = total.astype(bf16)
        start(quad_x(g))

    def pick(g, n, who):
        other = partner_ref[who]
        return [quads[g][c, lax.rem(other // 2, 2), lax.rem(other, 2)] for c in range(n)]

    def slab_far(g, n):
        arrived(quad_r(g))
        for k in range(1, 4):
            for c, value in enumerate(pick(g, n, lax.rem(r + 4 * k, 16))):
                ysends[g][k - 1, c] = value
        start(y_x(g))
        for c, value in enumerate(pick(g, n, r)):
            yalls[g][0, c] = value

    away = lax.rem(y - partner_ref[r] // 4 + 4, 4)

    def diff_near(g):
        arrived(y_x(g))
        first, count = groups[g]
        for c in range(count):
            own = quads[g][c, zl, core].astype(f32)
            dfull[first + c, :, mine] = (own - yalls[g][away, c].astype(f32)).astype(bf16)
        start(diff_z(g))

    def diff_far(g):
        arrived(diff_zr(g))
        start(diff_x(g))

    def gram_side(g):
        arrived(diff_xr(g))
        first, count = groups[g]
        for c in range(first, first + count):
            d = dfull[c]
            gram = dot_nt(d, d)
            side = dot_nn(d, gsend[c])
            if c == 0:
                gacc[...] = gram
                sacc[...] = side
            else:
                gacc[...] = gacc[...] + gram
                sacc[...] = sacc[...] + side

    def side_near():
        quad2[0, zl, core, pl.ds(0, 32)] = sacc[pl.ds(0, 32), pl.ds(0, HC)].astype(bf16)
        quad2[0, zl, core, pl.ds(32, 32)] = sacc[pl.ds(32, 32), pl.ds(HC, HC)].astype(bf16)
        start(quad_x(2))

    def inverses(mats):
        row_at = lax.broadcasted_iota(jnp.int32, (32, 32), 0)
        col_at = lax.broadcasted_iota(jnp.int32, (32, 32), 1)
        for k in range(32):
            step = []
            for m in mats:
                inv = 1.0 / m[k : k + 1, k : k + 1]
                row = jnp.where(col_at[:1] == k, inv, m[k : k + 1] * inv)
                col = m[:, k : k + 1]
                step.append(jnp.where(row_at == k, row, jnp.where(col_at == k, 0.0, m) - col * row))
            mats = step
        return mats

    def solve():
        gram = gacc[...]
        inv = inverses([gram[:32, :32], gram[32:, 32:]])
        arrived(y_x(2))
        other = yall2[away, 0].astype(f32)
        xhi[...] = jnp.zeros_like(xhi)
        xlo[...] = jnp.zeros_like(xlo)
        for a in range(2):
            rows, cols = pl.ds(a * 32, 32), pl.ds(a * HC, HC)
            total = sacc[rows, cols] + other[a * 32 : a * 32 + 32]
            x_a = 0.5 * lax.dot_general(
                inv[a], total, (((1,), (0,)), ((), ())),
                precision=lax.Precision.HIGHEST, preferred_element_type=f32,
            )
            high = x_a.astype(bf16)
            xhi[rows, cols] = high
            xlo[rows, cols] = (x_a - high.astype(f32)).astype(bf16)

    new_cp = [
        lcopy(gown.at[c, :, pl.ds(a * HC, HC)], (nk_o, nv_o)[a].at[0, pl.ds(c * CH, CH)], out_s.at[NC + 2 * c + a])
        for c in range(NC) for a in range(2)
    ]

    def renew(c):
        @pl.loop(0, CH // 256)
        def _(i):
            cols = pl.ds(pl.multiple_of(i * 256, 256), 256)
            rows = pl.ds(i * 256, 256)
            lhs = dfull[c, :, cols]
            gown[c, rows] = gown[c, rows] - (dot_tn(lhs, xhi[...]) + dot_tn(lhs, xlo[...]))

        new_cp[2 * c].start()
        new_cp[2 * c + 1].start()

    send_h(0)
    for cp in dk_x:
        cp.start()
    send_h(1)
    convert_w(0)
    w_x[0].start()
    for c in (0, 1):
        for cp in ad_loc[c]:
            cp.start()
    def arrive(c):
        forward_h(c)
        if c + 2 < NC:
            send_h(c + 2)
        if c + 1 < NC:
            convert_w(c + 1)
        if c == 0:
            for cp in dk_loc:
                cp.wait()
            for cp in dk_x:
                cp.wait_recv()
        grads(c)

    ko = []
    kx = []
    for s in range(4):
        for a in range(2):
            o = (keys_o, vals_o)[a].at[sl[s], z]
            kx.append(rcopy(kst.at[1, s, :, pl.ds(a * HC, HC)], o, ks_s.at[s, a], kr_s.at[s, a], pair))
            ko.append(lcopy(kst.at[0, s, :, pl.ds(a * HC, HC)], o, ko_s.at[s, a]))

    def keys_send(first, last):
        for cp in kx[first:last] + ko[first:last]:
            cp.start()

    arrive(0)
    g_x[0].start()
    arrive(1)
    g_x[1].start()
    w_x[1].start()
    adam(0)
    arrive(2)
    g_x[2].start()
    adam(1)
    arrive(3)
    g_x[3].start()
    arrive(4)
    g_x[4].start()
    terms_first(0)
    adam(2)
    panel_x(0)
    produce(0)
    terms_first(1)
    terms_second(0)
    panel_z(0)
    w_x[2].start()
    adam(3)
    produce(1)
    adam(4)
    panel_x(1)
    slab_near(0)
    terms_second(1)
    terms_last(0)
    slab_far(0, 3)
    panel_z(1)
    w_x[3].start()
    terms_first(2)
    diff_near(0)
    slab_near(1)
    w_x[4].start()
    terms_second(2)
    terms_last(1)
    produce(2)
    slab_far(1, 2)
    diff_far(0)
    diff_near(1)
    terms_first(3)
    terms_second(3)
    terms_last(2)
    gram_side(0)
    diff_far(1)
    produce(3)
    gram_side(1)
    side_near()
    terms_first(4)
    slab_far(2, 1)
    produce(4)
    keys_send(0, 8)
    terms_second(4)
    terms_last(3)
    solve()
    for c in range(NC):
        renew(c)
    terms_last(4)

    for cps in (h_r, h_l, f_r, f_l, dk_x, w_x, t1_r, t1_l, t2_r, t2_l, kx):
        for cp in cps:
            cp.wait_send()
    for cp in kx:
        cp.wait_recv()
    for cp in ko:
        cp.wait()
    for cp in ig_cp + new_cp:
        cp.wait()

    for g in range(2):
        for cps in (pan_x(g), pan_z(g), diff_z(g), diff_x(g)):
            for cp in cps:
                cp.wait_send()
    for g in range(3):
        for cp in quad_x(g) + y_x(g):
            cp.wait_send()


def gossip_round(h, wk, wv, mk, mv, sk, sv, gk, gv, start, partner):
    dma = pltpu.SemaphoreType.DMA
    any_spec = pl.BlockSpec(memory_space=pl.ANY)
    shapes = (
        jax.ShapeDtypeStruct((4, 2, RB, HC), bf16),
        jax.ShapeDtypeStruct((4, 2, RB, HC), bf16),
        jax.ShapeDtypeStruct((RB, NC * CH), bf16),
        jax.ShapeDtypeStruct((1, NC * CH, HC), f32),
        jax.ShapeDtypeStruct((1, NC * CH, HC), f32),
    )
    scratch = [
        pltpu.VMEM((NC, 4, RB, CH), bf16),
        pltpu.VMEM((NC, 2, CH, 2 * HC), bf16),
        pltpu.VMEM((2, 4, RB, 2 * HC), bf16),
        pltpu.VMEM((NC, CH, 2 * HC), f32),
        pltpu.VMEM((NC, CH, 2 * HC), bf16),
        pltpu.VMEM((NC, CH, 2 * HC), bf16),
        pltpu.VMEM((2, 2, CH, HC), f32),
        pltpu.VMEM((2, 3, 2, CH, HC), f32),
        pltpu.VMEM((NC, 4, RB, CH), bf16),
        pltpu.VMEM((NC, 2, HR, CH), bf16),
        pltpu.VMEM((NC, 2, RB, CH), bf16),
        pltpu.VMEM((2, 4, RB, 2 * HC), f32),
        pltpu.VMEM((2, 4, RB, 2 * HC), bf16),
        pltpu.VMEM((NC, 8, 64, HC), bf16),
        pltpu.VMEM((NC, 3, 2, 64, HC), bf16),
        pltpu.VMEM((NC, 64, HC), bf16),
        pltpu.VMEM((NC, 64, HC), bf16),
        *[pltpu.VMEM((n, 2, 2, 64, HC), bf16) for n in (3, 2, 1)],
        *[pltpu.VMEM((3, n, 64, HC), bf16) for n in (3, 2, 1)],
        *[pltpu.VMEM((4, n, 64, HC), bf16) for n in (3, 2, 1)],
        pltpu.VMEM((NC, 64, CH), bf16),
        pltpu.VMEM((64, 64), f32),
        pltpu.VMEM((64, 2 * HC), f32),
        pltpu.VMEM((64, 2 * HC), bf16),
        pltpu.VMEM((64, 2 * HC), bf16),
        dma((NC,)), dma((NC, 2)), dma((NC, 2)), dma((NC, 2)), dma((NC, 2)),
        dma((4, 2)), dma((4, 2)), dma((4, 2)), dma((2, 2)), dma((NC,)), dma((NC,)),
        dma((NC,)), dma((NC,)), dma((2, 3, 2)),
        dma((NC, 2)), dma((NC, 2)), dma((NC, 2)), dma((NC, 2)),
        dma((4, 2)), dma((4, 2)), dma((4, 2)), dma((3 * NC,)),
        dma((2, 4)), dma((2, 4)), dma((2,)), dma((2,)), dma((3, 3)), dma((3, 3)),
        dma((3, 4)), dma((3, 4)), dma((2,)), dma((2,)), dma((2, 4)), dma((2, 4)),
    ]
    return pl.pallas_call(
        round_kernel,
        out_shape=shapes,
        in_specs=[any_spec] * 9
        + [pl.BlockSpec(memory_space=pltpu.VMEM), pl.BlockSpec(memory_space=pltpu.SMEM)],
        out_specs=[any_spec] * 5,
        scratch_shapes=scratch,
        compiler_params=pltpu.CompilerParams(
            collective_id=0, has_side_effects=True, vmem_limit_bytes=60 << 20
        ),
        cost_estimate=pl.CostEstimate(flops=13_000_000_000, bytes_accessed=60_000_000, transcendentals=0),
        name="gossip_round",
    )(h, wk, wv, mk, mv, sk, sv, gk, gv, start, partner)


def body(hidden, w_key, w_value, moment_key, moment_value, second_key, second_value,
         grad_keys, grad_values, seed_panels, partner):
    seeds = jnp.transpose(seed_panels, (0, 2, 1)).astype(bf16)
    zero = jnp.zeros_like(seeds[0])
    start = jnp.concatenate(
        [jnp.concatenate([seeds[0], zero], 1), jnp.concatenate([zero, seeds[1]], 1)], 0
    )
    keys, values, input_grad, new_key, new_value = gossip_round(
        hidden, w_key, w_value, moment_key, moment_value, second_key, second_value,
        grad_keys.reshape(4, 2, RB, HC), grad_values.reshape(4, 2, RB, HC), start, partner,
    )
    return keys.reshape(8 * RB, HC), values.reshape(8 * RB, HC), input_grad, new_key, new_value


def solution(mesh):
    return jax.shard_map(
        body,
        mesh=mesh,
        in_specs=(
            P(("replica", "tensor"), None),
            P("replica", None, "tensor"),
            P("replica", None, "tensor"),
            P("replica", None, "tensor"),
            P("replica", None, "tensor"),
            P("replica", None, "tensor"),
            P("replica", None, "tensor"),
            P("replica", "tensor"),
            P("replica", "tensor"),
            P(None, "tensor", None),
            P(),
        ),
        out_specs=(
            P("replica", "tensor"),
            P("replica", "tensor"),
            P(("replica", "tensor"), None),
            P("replica", None, "tensor"),
            P("replica", None, "tensor"),
        ),
        check_vma=False,
    )
```

```python
import functools
import jax
import jax.numpy as jnp
from jax import lax
from jax.experimental import pallas as pl
from jax.experimental.pallas import tpu as pltpu
from jax.sharding import PartitionSpec as P

MESH = pl.DeviceIdType.MESH
beta_one = 0.9
beta_two = 0.95
epsilon = 1e-08
learn_rate = 0.06
decay_rate = 0.1
step_count = 100.0

NC = 5
CH = 1024
PIECES = ((0, 0, CH), (1, 0, CH), (2, 0, CH), (3, 0, CH), (4, 0, CH // 2), (4, CH // 2, CH // 2))
NP = len(PIECES)
RB = 192
HR = 96
HC = 128
bf16 = jnp.bfloat16
f32 = jnp.float32


def slots(x):
    return (x, lax.rem(x + 3, 4), lax.rem(x + 1, 4), lax.rem(x + 2, 4))


def dot_tn(a, b):
    return lax.dot_general(a, b, (((0,), (0,)), ((), ())), preferred_element_type=f32)


def dot_nt(a, b):
    return lax.dot_general(a, b, (((1,), (1,)), ((), ())), preferred_element_type=f32)


def dot_nn(a, b):
    return lax.dot_general(a, b, (((1,), (0,)), ((), ())), preferred_element_type=f32)


def round_kernel(
    h_ref, wk_ref, wv_ref, mk_ref, mv_ref, sk_ref, sv_ref, gk_ref, gv_ref, seed_ref, partner_ref,
    keys_o, vals_o, ig_o, ad_o, df_o, xs_o,
    hz, wp, dk, gown, gsend, grecv, wcv, adin, ts, trh, trf, kacc, kst,
    pan, prx, psend, prz, quad0, quad1, quad2, ysend0, ysend1, ysend2, yall0, yall1, yall2,
    st, dfull, gacc, sacc, xs,
    lh_s, hs_s, hr_s, fs_s, fr_s, ldk_s, dks_s, dkr_s, lw_s, ws_s, wr_s, gs_s, gr_s,
    lad_s, t1s_s, t1r_s, t2s_s, t2r_s, ig_s, ko_s, ks_s, kr_s, out_s,
    px_s, px_r, pz_s, pz_r, qs_s, qr_s, ys_s, yr_s, dz_s, dz_r, dx_s, dx_r,
):
    r = lax.axis_index("replica")
    t = lax.axis_index("tensor")
    x = t // 2
    z = lax.rem(t, 2)
    right = (r, lax.rem(x + 1, 4) * 2 + z)
    left = (r, lax.rem(x + 3, 4) * 2 + z)
    pair = (r, x * 2 + (1 - z))
    sl = slots(x)
    quads, ysends, yalls = (quad0, quad1, quad2), (ysend0, ysend1, ysend2), (yall0, yall1, yall2)
    y = r // 4
    zl = lax.rem(r // 2, 2)
    core = lax.rem(r, 2)
    near = (
        (y * 4 + zl * 2 + 1 - core, t),
        (y * 4 + (1 - zl) * 2 + core, t),
        (y * 4 + (1 - zl) * 2 + 1 - core, t),
    )
    g_refs = (gk_ref, gv_ref)
    w_refs = (wk_ref, wv_ref)
    ad_refs = ((wk_ref, wv_ref), (mk_ref, mv_ref), (sk_ref, sv_ref))

    def rcopy(src, dst, ssem, rsem, dev):
        return pltpu.make_async_remote_copy(
            src_ref=src, dst_ref=dst, send_sem=ssem, recv_sem=rsem,
            device_id=dev, device_id_type=MESH,
        )

    def lcopy(src, dst, sem):
        return pltpu.make_async_copy(src, dst, sem)

    dk_loc = [
        lcopy(g_refs[a].at[sl[s], z], dk.at[0, s, :, pl.ds(a * HC, HC)], ldk_s.at[s, a])
        for s in range(4) for a in range(2)
    ]
    h_loc = [lcopy(h_ref.at[:, pl.ds(c * CH, CH)], hz.at[c, 0], lh_s.at[c]) for c in range(NC)]
    w_loc = [
        [lcopy(w_refs[a].at[0, pl.ds(c * CH, CH)], wcv.at[c % 2, a], lw_s.at[c % 2, a]) for a in range(2)]
        for c in range(NC)
    ]
    ad_loc = [
        [
            lcopy(ad_refs[k][a].at[0, pl.ds(c * CH, CH)], adin.at[c % 2, k, a], lad_s.at[c % 2, k, a])
            for k in range(3) for a in range(2)
        ]
        for c in range(NC)
    ]
    for c in (0, 1):
        for cp in w_loc[c]:
            cp.start()
    for cp in dk_loc:
        cp.start()
    for cp in h_loc:
        cp.start()

    st[...] = jnp.zeros_like(st)
    for a in range(2):
        st[pl.ds(a * 32, 32), pl.ds(a * HC, HC)] = seed_ref[a].astype(f32).astype(bf16)

    barrier = pltpu.get_barrier_semaphore()
    peers = [pair, *near]
    for k in range(1, 4):
        peers.append((r, lax.rem(x + k, 4) * 2 + z))
        peers.append((lax.rem(r + 4 * k, 16), t))
    for dev in peers:
        pl.semaphore_signal(barrier, inc=1, device_id=dev, device_id_type=MESH)
    pl.semaphore_wait(barrier, len(peers))

    h_r = [rcopy(h_ref.at[:, pl.ds(c * CH, CH)], hz.at[c, 1], hs_s.at[c, 0], hr_s.at[c, 0], right) for c in range(NC)]
    h_l = [rcopy(h_ref.at[:, pl.ds(c * CH, CH)], hz.at[c, 2], hs_s.at[c, 1], hr_s.at[c, 1], left) for c in range(NC)]
    f_r = [rcopy(hz.at[c, 1, pl.ds(0, HR)], hz.at[c, 3, pl.ds(0, HR)], fs_s.at[c, 0], fr_s.at[c, 0], right) for c in range(NC)]
    f_l = [rcopy(hz.at[c, 2, pl.ds(HR, HR)], hz.at[c, 3, pl.ds(HR, HR)], fs_s.at[c, 1], fr_s.at[c, 1], left) for c in range(NC)]
    dk_x = [
        rcopy(g_refs[a].at[sl[s], 1 - z], dk.at[1, s, :, pl.ds(a * HC, HC)], dks_s.at[s, a], dkr_s.at[s, a], pair)
        for s in range(4) for a in range(2)
    ]
    w_x = [
        rcopy(wp.at[c, 0, pl.ds(o, n)], wp.at[c, 1, pl.ds(o, n)], ws_s.at[q], wr_s.at[q], pair)
        for q, (c, o, n) in enumerate(PIECES)
    ]
    g_x = [rcopy(gsend.at[c], grecv.at[c], gs_s.at[c], gr_s.at[c], pair) for c in range(NC)]
    t1_r, t1_l, t2_r, t2_l = [], [], [], []
    for q, (c, o, n) in enumerate(PIECES):
        cols = pl.ds(o, n)
        t1_r.append(rcopy(ts.at[c, 3, pl.ds(0, HR), cols], trh.at[c, 0, :, cols], t1s_s.at[q, 0], t1r_s.at[q, 0], right))
        t1_l.append(rcopy(ts.at[c, 3, pl.ds(HR, HR), cols], trh.at[c, 1, :, cols], t1s_s.at[q, 1], t1r_s.at[q, 1], left))
        t2_r.append(rcopy(ts.at[c, 2, :, cols], trf.at[c, 0, :, cols], t2s_s.at[q, 0], t2r_s.at[q, 0], right))
        t2_l.append(rcopy(ts.at[c, 1, :, cols], trf.at[c, 1, :, cols], t2s_s.at[q, 1], t2r_s.at[q, 1], left))

    def send_h(c):
        h_r[c].start()
        h_l[c].start()

    def convert_w(c):
        for cp in w_loc[c]:
            cp.wait()

        @pl.loop(0, CH // 256)
        def _(i):
            rows = pl.ds(i * 256, 256)
            for a in range(2):
                wp[c, 0, rows, pl.ds(a * HC, HC)] = wcv[c % 2, a, rows].astype(bf16)

        if c + 2 < NC:
            for cp in w_loc[c + 2]:
                cp.start()

    def forward_h(c):
        h_r[c].wait_recv()
        f_r[c].start()
        h_l[c].wait_recv()
        f_l[c].start()

    def grads(c):
        h_loc[c].wait()
        f_r[c].wait_recv()
        f_l[c].wait_recv()

        @pl.loop(0, CH // 256)
        def _(i):
            cols = pl.ds(pl.multiple_of(i * 256, 256), 256)
            rows = pl.ds(i * 256, 256)
            lhs = hz[c, :, :, cols].reshape(4 * RB, 256).T
            gsend[c, rows] = dot_nn(lhs, dk[1].reshape(4 * RB, 2 * HC)).astype(bf16)
            gown[c, rows] = dot_nn(lhs, dk[0].reshape(4 * RB, 2 * HC))

    def produce(c):
        for p in range(2):
            add = dot_nn(hz[c].reshape(4 * RB, CH), wp[c, p]).reshape(4, RB, 2 * HC)
            if c == 0:
                kacc[p] = add
            elif c < NC - 1:
                kacc[p] = kacc[p] + add
            else:
                kst[p] = (kacc[p] + add).astype(bf16)

    def terms_first(q):
        c, o, n = PIECES[q]
        w_x[q].wait_recv()

        @pl.loop(0, n // 256)
        def _(i):
            cols = pl.ds(pl.multiple_of(o + i * 256, 256), 256)
            rows = pl.ds(pl.multiple_of(o + i * 256, 256), 256)
            total = dot_nt(dk[0].reshape(4 * RB, 2 * HC), wp[c, 0, rows])
            total = total + dot_nt(dk[1].reshape(4 * RB, 2 * HC), wp[c, 1, rows])
            ts[c, :, :, cols] = total.astype(bf16).reshape(4, RB, 256)

        t1_r[q].start()
        t1_l[q].start()

    def terms_second(q):
        c, o, n = PIECES[q]
        cols = pl.ds(o, n)
        low, high = pl.ds(0, HR), pl.ds(HR, HR)
        t1_r[q].wait_recv()
        ts[c, 2, low, cols] = (ts[c, 2, low, cols].astype(f32) + trh[c, 0, :, cols].astype(f32)).astype(bf16)
        t2_r[q].start()
        t1_l[q].wait_recv()
        ts[c, 1, high, cols] = (ts[c, 1, high, cols].astype(f32) + trh[c, 1, :, cols].astype(f32)).astype(bf16)
        t2_l[q].start()

    ig_cp = [
        lcopy(ts.at[c, 0, :, pl.ds(o, n)], ig_o.at[:, pl.ds(c * CH + o, n)], ig_s.at[q])
        for q, (c, o, n) in enumerate(PIECES)
    ]

    def terms_last(q):
        c, o, n = PIECES[q]
        cols = pl.ds(o, n)
        t2_r[q].wait_recv()
        t2_l[q].wait_recv()
        total = ts[c, 0, :, cols].astype(f32) + trf[c, 0, :, cols].astype(f32)
        ts[c, 0, :, cols] = (total + trf[c, 1, :, cols].astype(f32)).astype(bf16)
        ig_cp[q].start()

    first_scale = 1.0 / (1.0 - beta_one**step_count)
    second_scale = 1.0 / (1.0 - beta_two**step_count)

    def adam(c):
        g_x[c].wait()
        for cp in ad_loc[c]:
            cp.wait()

        @pl.loop(0, CH // 64)
        def _(i):
            rows = pl.ds(i * 64, 64)
            for a in range(2):
                cols = pl.ds(a * HC, HC)
                g = gown[c, rows, cols] + grecv[c, rows, cols].astype(f32)
                weight = adin[c % 2, 0, a, rows]
                moment = beta_one * adin[c % 2, 1, a, rows] + (1.0 - beta_one) * g
                second = beta_two * adin[c % 2, 2, a, rows] + (1.0 - beta_two) * g * g
                step = (moment * first_scale) / (jnp.sqrt(second * second_scale) + epsilon)
                new = weight - learn_rate * (step + decay_rate * weight)
                gown[c, rows, cols] = new
                gsend[c, rows, cols] = new.astype(bf16)

        if c + 2 < NC:
            for cp in ad_loc[c + 2]:
                cp.start()
        ad_cp[c].start()

        @pl.loop(0, CH // 256)
        def _(i):
            rows = pl.ds(i * 256, 256)
            tile = dot_nt(st[...], gsend[c, rows]).astype(bf16)
            pan[c, 2 * i] = tile[:, :HC]
            pan[c, 2 * i + 1] = tile[:, HC:]

    groups = ((0, 3), (3, 2))

    def chunks(g):
        return pl.ds(groups[g][0], groups[g][1])

    def pan_x(g):
        return [
            rcopy(
                pan.at[chunks(g), pl.ds(lax.rem(x + k, 4) * 2, 2)], prx.at[chunks(g), k - 1],
                px_s.at[g, k], px_r.at[g, k], (r, lax.rem(x + k, 4) * 2 + z),
            )
            for k in range(1, 4)
        ]

    def pan_z(g):
        return [rcopy(psend.at[chunks(g)], prz.at[chunks(g)], pz_s.at[g], pz_r.at[g], pair)]

    def quad_x(g):
        part = quads[g].at[:, zl, core]
        return [rcopy(part, part, qs_s.at[g, k], qr_s.at[g, k], near[k]) for k in range(3)]

    def quad_r(g):
        from_at = ((zl, 1 - core), (1 - zl, core), (1 - zl, 1 - core))
        return [
            rcopy(quads[g].at[:, a, b], quads[g].at[:, a, b], qs_s.at[g, k], qr_s.at[g, k], near[k])
            for k, (a, b) in enumerate(from_at)
        ]

    def y_x(g):
        return [
            rcopy(
                ysends[g].at[k - 1], yalls[g].at[k], ys_s.at[g, k], yr_s.at[g, k],
                (lax.rem(r + 4 * k, 16), t),
            )
            for k in range(1, 4)
        ]

    mine = pl.ds(pl.multiple_of(t * HC, HC), HC)

    def both(at):
        return pl.ds(pl.multiple_of(at * 2 * HC, 2 * HC), 2 * HC)

    def diff_z(g):
        part = dfull.at[chunks(g), :, mine]
        return [rcopy(part, part, dz_s.at[g], dz_r.at[g], pair)]

    def diff_zr(g):
        part = dfull.at[chunks(g), :, pl.ds(pl.multiple_of((x * 2 + 1 - z) * HC, HC), HC)]
        return [rcopy(part, part, dz_s.at[g], dz_r.at[g], pair)]

    def diff_x(g):
        part = dfull.at[chunks(g), :, both(x)]
        return [
            rcopy(part, part, dx_s.at[g, k], dx_r.at[g, k], (r, lax.rem(x + k, 4) * 2 + z))
            for k in range(1, 4)
        ]

    def diff_xr(g):
        out = []
        for k in range(1, 4):
            part = dfull.at[chunks(g), :, both(lax.rem(x + 4 - k, 4))]
            out.append(rcopy(part, part, dx_s.at[g, k], dx_r.at[g, k], (r, lax.rem(x + k, 4) * 2 + z)))
        return out

    def start(cps):
        for cp in cps:
            cp.start()

    def arrived(cps):
        for cp in cps:
            cp.wait_recv()

    def panel_x(g):
        start(pan_x(g))

    def panel_z(g):
        arrived(pan_x(g))
        first, count = groups[g]
        for c in range(first, first + count):
            total = pan[c, x * 2 + 1 - z].astype(f32)
            for k in range(3):
                total = total + prx[c, k, 1 - z].astype(f32)
            psend[c] = total.astype(bf16)
        start(pan_z(g))

    def slab_near(g):
        arrived(pan_z(g))
        first, count = groups[g]
        for c in range(first, first + count):
            total = pan[c, t].astype(f32) + prz[c].astype(f32)
            for k in range(3):
                total = total + prx[c, k, z].astype(f32)
            quads[g][c - first, zl, core] = total.astype(bf16)
        start(quad_x(g))

    def pick(g, n, who):
        other = partner_ref[who]
        return [quads[g][c, lax.rem(other // 2, 2), lax.rem(other, 2)] for c in range(n)]

    def slab_far(g, n):
        arrived(quad_r(g))
        for k in range(1, 4):
            for c, value in enumerate(pick(g, n, lax.rem(r + 4 * k, 16))):
                ysends[g][k - 1, c] = value
        start(y_x(g))
        for c, value in enumerate(pick(g, n, r)):
            yalls[g][0, c] = value

    away = lax.rem(y - partner_ref[r] // 4 + 4, 4)

    def diff_near(g):
        arrived(y_x(g))
        first, count = groups[g]
        for c in range(count):
            own = quads[g][c, zl, core].astype(f32)
            dfull[first + c, :, mine] = (own - yalls[g][away, c].astype(f32)).astype(bf16)
        start(diff_z(g))

    def diff_far(g):
        arrived(diff_zr(g))
        start(diff_x(g))

    def gram_side(g):
        arrived(diff_xr(g))
        first, count = groups[g]
        for c in range(first, first + count):
            d = dfull[c]
            gram = dot_nt(d, d)
            side = dot_nn(d, gsend[c])
            if c == 0:
                gacc[...] = gram
                sacc[...] = side
            else:
                gacc[...] = gacc[...] + gram
                sacc[...] = sacc[...] + side

    def side_near():
        quad2[0, zl, core, pl.ds(0, 32)] = sacc[pl.ds(0, 32), pl.ds(0, HC)].astype(bf16)
        quad2[0, zl, core, pl.ds(32, 32)] = sacc[pl.ds(32, 32), pl.ds(HC, HC)].astype(bf16)
        start(quad_x(2))

    def inverses(mats):
        row_at = lax.broadcasted_iota(jnp.int32, (32, 32), 0)
        col_at = lax.broadcasted_iota(jnp.int32, (32, 32), 1)
        for k in range(32):
            step = []
            for m in mats:
                inv = 1.0 / m[k : k + 1, k : k + 1]
                row = jnp.where(col_at[:1] == k, inv, m[k : k + 1] * inv)
                col = m[:, k : k + 1]
                step.append(jnp.where(row_at == k, row, jnp.where(col_at == k, 0.0, m) - col * row))
            mats = step
        return mats

    def gram_inverses():
        return inverses([gacc[pl.ds(0, 32), pl.ds(0, 32)], gacc[pl.ds(32, 32), pl.ds(32, 32)]])

    def solve(inv):
        arrived(y_x(2))
        other = yall2[away, 0].astype(f32)
        xs[...] = jnp.zeros_like(xs)
        for a in range(2):
            rows, cols = pl.ds(a * 32, 32), pl.ds(a * HC, HC)
            total = sacc[rows, cols] + other[a * 32 : a * 32 + 32]
            xs[rows, cols] = 0.5 * lax.dot_general(
                inv[a], total, (((1,), (0,)), ((), ())),
                precision=lax.Precision.HIGHEST, preferred_element_type=f32,
            )
        xs_cp.start()

    ad_cp = [lcopy(gown.at[c], ad_o.at[c], out_s.at[NC + c]) for c in range(NC)]
    df_cp = lcopy(dfull, df_o, out_s.at[2 * NC])
    xs_cp = lcopy(xs, xs_o, out_s.at[2 * NC + 1])

    send_h(0)
    for cp in dk_x:
        cp.start()
    send_h(1)
    convert_w(0)
    w_x[0].start()
    for c in (0, 1):
        for cp in ad_loc[c]:
            cp.start()

    def arrive(c):
        forward_h(c)
        if c + 2 < NC:
            send_h(c + 2)
        if c + 1 < NC:
            convert_w(c + 1)
        if c == 0:
            for cp in dk_loc:
                cp.wait()
            for cp in dk_x:
                cp.wait_recv()
        grads(c)

    ko = []
    kx = []
    for s in range(4):
        for a in range(2):
            o = (keys_o, vals_o)[a].at[sl[s], z]
            kx.append(rcopy(kst.at[1, s, :, pl.ds(a * HC, HC)], o, ks_s.at[s, a], kr_s.at[s, a], pair))
            ko.append(lcopy(kst.at[0, s, :, pl.ds(a * HC, HC)], o, ko_s.at[s, a]))

    def keys_send(first, last):
        for cp in kx[first:last] + ko[first:last]:
            cp.start()

    arrive(0)
    g_x[0].start()
    arrive(1)
    g_x[1].start()
    w_x[1].start()
    adam(0)
    arrive(2)
    g_x[2].start()
    adam(1)
    arrive(3)
    g_x[3].start()
    arrive(4)
    g_x[4].start()
    terms_first(0)
    adam(2)
    panel_x(0)
    produce(0)
    terms_first(1)
    terms_second(0)
    panel_z(0)
    w_x[2].start()
    adam(3)
    produce(1)
    adam(4)
    panel_x(1)
    slab_near(0)
    terms_second(1)
    terms_last(0)
    panel_z(1)
    w_x[3].start()
    terms_first(2)
    slab_near(1)
    slab_far(0, 3)
    terms_second(2)
    terms_last(1)
    produce(2)
    diff_near(0)
    w_x[4].start()
    w_x[5].start()
    terms_first(3)
    slab_far(1, 2)
    diff_far(0)
    diff_near(1)
    terms_second(3)
    terms_last(2)
    produce(3)
    diff_far(1)
    terms_first(4)
    gram_side(0)
    terms_first(5)
    produce(4)
    keys_send(0, 8)
    terms_second(4)
    terms_last(3)
    gram_side(1)
    df_cp.start()
    side_near()
    terms_second(5)
    inv = gram_inverses()
    slab_far(2, 1)
    terms_last(4)
    solve(inv)
    terms_last(5)

    for cps in (h_r, h_l, f_r, f_l, dk_x, w_x, t1_r, t1_l, t2_r, t2_l, kx):
        for cp in cps:
            cp.wait_send()
    for cp in kx:
        cp.wait_recv()
    for cp in ko:
        cp.wait()
    for cp in ig_cp + ad_cp + [df_cp, xs_cp]:
        cp.wait()

    for g in range(2):
        for cps in (pan_x(g), pan_z(g), diff_z(g), diff_x(g)):
            for cp in cps:
                cp.wait_send()
    for g in range(3):
        for cp in quad_x(g) + y_x(g):
            cp.wait_send()


def gossip_round(h, wk, wv, mk, mv, sk, sv, gk, gv, start, partner):
    dma = pltpu.SemaphoreType.DMA
    any_spec = pl.BlockSpec(memory_space=pl.ANY)
    shapes = (
        jax.ShapeDtypeStruct((4, 2, RB, HC), bf16),
        jax.ShapeDtypeStruct((4, 2, RB, HC), bf16),
        jax.ShapeDtypeStruct((RB, NC * CH), bf16),
        jax.ShapeDtypeStruct((NC, CH, 2 * HC), f32),
        jax.ShapeDtypeStruct((NC, 64, CH), bf16),
        jax.ShapeDtypeStruct((64, 2 * HC), f32),
    )
    scratch = [
        pltpu.VMEM((NC, 4, RB, CH), bf16),
        pltpu.VMEM((NC, 2, CH, 2 * HC), bf16),
        pltpu.VMEM((2, 4, RB, 2 * HC), bf16),
        pltpu.VMEM((NC, CH, 2 * HC), f32),
        pltpu.VMEM((NC, CH, 2 * HC), bf16),
        pltpu.VMEM((NC, CH, 2 * HC), bf16),
        pltpu.VMEM((2, 2, CH, HC), f32),
        pltpu.VMEM((2, 3, 2, CH, HC), f32),
        pltpu.VMEM((NC, 4, RB, CH), bf16),
        pltpu.VMEM((NC, 2, HR, CH), bf16),
        pltpu.VMEM((NC, 2, RB, CH), bf16),
        pltpu.VMEM((2, 4, RB, 2 * HC), f32),
        pltpu.VMEM((2, 4, RB, 2 * HC), bf16),
        pltpu.VMEM((NC, 8, 64, HC), bf16),
        pltpu.VMEM((NC, 3, 2, 64, HC), bf16),
        pltpu.VMEM((NC, 64, HC), bf16),
        pltpu.VMEM((NC, 64, HC), bf16),
        *[pltpu.VMEM((n, 2, 2, 64, HC), bf16) for n in (3, 2, 1)],
        *[pltpu.VMEM((3, n, 64, HC), bf16) for n in (3, 2, 1)],
        *[pltpu.VMEM((4, n, 64, HC), bf16) for n in (3, 2, 1)],
        pltpu.VMEM((64, 2 * HC), bf16),
        pltpu.VMEM((NC, 64, CH), bf16),
        pltpu.VMEM((64, 64), f32),
        pltpu.VMEM((64, 2 * HC), f32),
        pltpu.VMEM((64, 2 * HC), f32),
        dma((NC,)), dma((NC, 2)), dma((NC, 2)), dma((NC, 2)), dma((NC, 2)),
        dma((4, 2)), dma((4, 2)), dma((4, 2)), dma((2, 2)), dma((NP,)), dma((NP,)),
        dma((NC,)), dma((NC,)), dma((2, 3, 2)),
        dma((NP, 2)), dma((NP, 2)), dma((NP, 2)), dma((NP, 2)), dma((NP,)),
        dma((4, 2)), dma((4, 2)), dma((4, 2)), dma((2 * NC + 2,)),
        dma((2, 4)), dma((2, 4)), dma((2,)), dma((2,)), dma((3, 3)), dma((3, 3)),
        dma((3, 4)), dma((3, 4)), dma((2,)), dma((2,)), dma((2, 4)), dma((2, 4)),
    ]
    return pl.pallas_call(
        round_kernel,
        out_shape=shapes,
        in_specs=[any_spec] * 9
        + [pl.BlockSpec(memory_space=pltpu.VMEM), pl.BlockSpec(memory_space=pltpu.SMEM)],
        out_specs=[any_spec] * 6,
        scratch_shapes=scratch,
        compiler_params=pltpu.CompilerParams(
            collective_id=0, has_side_effects=True, vmem_limit_bytes=60 << 20
        ),
        cost_estimate=pl.CostEstimate(flops=13_000_000_000, bytes_accessed=60_000_000, transcendentals=0),
        name="gossip_round",
    )(h, wk, wv, mk, mv, sk, sv, gk, gv, start, partner)


def renew_kernel(k_ref, v_ref, i_ref, ad_ref, df_ref, x_ref, k_o, v_o, i_o, nk_o, nv_o, held, sems):
    step = pl.program_id(0)
    loads = [pltpu.make_async_copy(a, held.at[n], sems.at[n]) for n, a in enumerate((k_ref, v_ref))]
    stores = [pltpu.make_async_copy(held.at[n], a, sems.at[2 + n]) for n, a in enumerate((k_o, v_o))]

    @pl.when(step == 0)
    def _():
        for cp in loads:
            cp.start()

    @pl.when(step == 1)
    def _():
        for cp in loads:
            cp.wait()
        for cp in stores:
            cp.start()

    i_o[...] = i_ref[...]
    high = x_ref[...].astype(bf16)
    low = (x_ref[...] - high.astype(f32)).astype(bf16)

    @pl.loop(0, CH // 256)
    def _(i):
        cols = pl.ds(pl.multiple_of(i * 256, 256), 256)
        rows = pl.ds(i * 256, 256)
        lhs = df_ref[0, :, cols].T
        new = ad_ref[0, rows] - (dot_nn(lhs, high) + dot_nn(lhs, low))
        nk_o[0, rows] = new[:, :HC]
        nv_o[0, rows] = new[:, HC:]

    @pl.when(step == NC - 1)
    def _():
        for cp in stores:
            cp.wait()


def renew(keys, values, input_grad, adapted, diff, panels):
    any_spec = pl.BlockSpec(memory_space=pl.ANY)
    new_spec = pl.BlockSpec((1, CH, HC), lambda c: (0, c, 0))
    ig_spec = pl.BlockSpec((RB, CH), lambda c: (0, c))
    new_shape = jax.ShapeDtypeStruct((1, NC * CH, HC), f32)
    return pl.pallas_call(
        renew_kernel,
        grid=(NC,),
        out_shape=(
            jax.ShapeDtypeStruct(keys.shape, bf16),
            jax.ShapeDtypeStruct(values.shape, bf16),
            jax.ShapeDtypeStruct(input_grad.shape, bf16),
            new_shape, new_shape,
        ),
        in_specs=[any_spec, any_spec, ig_spec,
            pl.BlockSpec((1, CH, 2 * HC), lambda c: (c, 0, 0)),
            pl.BlockSpec((1, 64, CH), lambda c: (c, 0, 0)),
            pl.BlockSpec((64, 2 * HC), lambda c: (0, 0)),
        ],
        out_specs=[any_spec, any_spec, ig_spec, new_spec, new_spec],
        scratch_shapes=[pltpu.VMEM((2, 8 * RB, HC), bf16), pltpu.SemaphoreType.DMA((4,))],
        compiler_params=pltpu.CompilerParams(vmem_limit_bytes=60 << 20),
        cost_estimate=pl.CostEstimate(flops=400_000_000, bytes_accessed=17_000_000, transcendentals=0),
        name="renew",
    )(keys, values, input_grad, adapted, diff, panels)


def body(hidden, w_key, w_value, moment_key, moment_value, second_key, second_value,
         grad_keys, grad_values, seed_panels, partner):
    start = jnp.transpose(seed_panels, (0, 2, 1))
    keys, values, input_grad, adapted, diff, panels = gossip_round(
        hidden, w_key, w_value, moment_key, moment_value, second_key, second_value,
        grad_keys.reshape(4, 2, RB, HC), grad_values.reshape(4, 2, RB, HC), start, partner,
    )
    keys, values, input_grad, new_key, new_value = renew(
        keys.reshape(8 * RB, HC), values.reshape(8 * RB, HC), input_grad, adapted, diff, panels
    )
    return keys, values, input_grad, new_key, new_value


def solution(mesh):
    return jax.shard_map(
        body,
        mesh=mesh,
        in_specs=(
            P(("replica", "tensor"), None),
            P("replica", None, "tensor"),
            P("replica", None, "tensor"),
            P("replica", None, "tensor"),
            P("replica", None, "tensor"),
            P("replica", None, "tensor"),
            P("replica", None, "tensor"),
            P("replica", "tensor"),
            P("replica", "tensor"),
            P(None, "tensor", None),
            P(),
        ),
        out_specs=(
            P("replica", "tensor"),
            P("replica", "tensor"),
            P(("replica", "tensor"), None),
            P("replica", None, "tensor"),
            P("replica", None, "tensor"),
        ),
        check_vma=False,
    )
```

```python
import functools
import jax
import jax.numpy as jnp
from jax import lax
from jax.experimental import pallas as pl
from jax.experimental.pallas import tpu as pltpu
from jax.sharding import PartitionSpec as P

MESH = pl.DeviceIdType.MESH
beta_one = 0.9
beta_two = 0.95
epsilon = 1e-08
learn_rate = 0.06
decay_rate = 0.1
step_count = 100.0

NC = 5
CH = 1024
PIECES = ((0, 0, CH), (1, 0, CH), (2, 0, CH), (3, 0, CH), (4, 0, CH // 2), (4, CH // 2, CH // 2))
NP = len(PIECES)
RB = 192
HR = 96
HC = 128
bf16 = jnp.bfloat16
f32 = jnp.float32


def slots(x):
    return (x, lax.rem(x + 3, 4), lax.rem(x + 1, 4), lax.rem(x + 2, 4))


def dot_tn(a, b):
    return lax.dot_general(a, b, (((0,), (0,)), ((), ())), preferred_element_type=f32)


def dot_nt(a, b):
    return lax.dot_general(a, b, (((1,), (1,)), ((), ())), preferred_element_type=f32)


def dot_nn(a, b):
    return lax.dot_general(a, b, (((1,), (0,)), ((), ())), preferred_element_type=f32)


def round_kernel(
    h_ref, wk_ref, wv_ref, mk_ref, mv_ref, sk_ref, sv_ref, gk_ref, gv_ref, seed_ref, partner_ref,
    keys_o, vals_o, ig_o, ad_o, df_o, xs_o,
    hz, wp, dk, gown, gsend, grecv, wcv, adin, ts, trh, trf, kacc, kst,
    pan, prx, psend, prz, quad0, quad1, quad2, ysend0, ysend1, ysend2, yall0, yall1, yall2,
    st, dfull, gacc, sacc, xs,
    lh_s, hs_s, hr_s, fs_s, fr_s, ldk_s, dks_s, dkr_s, lw_s, ws_s, wr_s, gs_s, gr_s,
    lad_s, t1s_s, t1r_s, t2s_s, t2r_s, ig_s, ko_s, ks_s, kr_s, out_s,
    px_s, px_r, pz_s, pz_r, qs_s, qr_s, ys_s, yr_s, dz_s, dz_r, dx_s, dx_r,
):
    r = lax.axis_index("replica")
    t = lax.axis_index("tensor")
    x = t // 2
    z = lax.rem(t, 2)
    right = (r, lax.rem(x + 1, 4) * 2 + z)
    left = (r, lax.rem(x + 3, 4) * 2 + z)
    pair = (r, x * 2 + (1 - z))
    sl = slots(x)
    quads, ysends, yalls = (quad0, quad1, quad2), (ysend0, ysend1, ysend2), (yall0, yall1, yall2)
    y = r // 4
    zl = lax.rem(r // 2, 2)
    core = lax.rem(r, 2)
    near = (
        (y * 4 + zl * 2 + 1 - core, t),
        (y * 4 + (1 - zl) * 2 + core, t),
        (y * 4 + (1 - zl) * 2 + 1 - core, t),
    )
    g_refs = (gk_ref, gv_ref)
    w_refs = (wk_ref, wv_ref)
    ad_refs = ((wk_ref, wv_ref), (mk_ref, mv_ref), (sk_ref, sv_ref))

    def rcopy(src, dst, ssem, rsem, dev):
        return pltpu.make_async_remote_copy(
            src_ref=src, dst_ref=dst, send_sem=ssem, recv_sem=rsem,
            device_id=dev, device_id_type=MESH,
        )

    def lcopy(src, dst, sem):
        return pltpu.make_async_copy(src, dst, sem)

    dk_loc = [
        lcopy(g_refs[a].at[sl[s], z], dk.at[0, s, :, pl.ds(a * HC, HC)], ldk_s.at[s, a])
        for s in range(4) for a in range(2)
    ]
    h_loc = [lcopy(h_ref.at[:, pl.ds(c * CH, CH)], hz.at[c, 0], lh_s.at[c]) for c in range(NC)]
    w_loc = [
        [lcopy(w_refs[a].at[0, pl.ds(c * CH, CH)], wcv.at[c % 2, a], lw_s.at[c % 2, a]) for a in range(2)]
        for c in range(NC)
    ]
    ad_loc = [
        [
            lcopy(ad_refs[k][a].at[0, pl.ds(c * CH, CH)], adin.at[c % 2, k, a], lad_s.at[c % 2, k, a])
            for k in range(3) for a in range(2)
        ]
        for c in range(NC)
    ]
    for c in (0, 1):
        for cp in w_loc[c]:
            cp.start()
    for cp in dk_loc:
        cp.start()
    for cp in h_loc:
        cp.start()

    st[...] = jnp.zeros_like(st)
    for a in range(2):
        st[pl.ds(a * 32, 32), pl.ds(a * HC, HC)] = seed_ref[a].astype(f32).astype(bf16)

    barrier = pltpu.get_barrier_semaphore()
    peers = [pair, *near]
    for k in range(1, 4):
        peers.append((r, lax.rem(x + k, 4) * 2 + z))
        peers.append((lax.rem(r + 4 * k, 16), t))
    for dev in peers:
        pl.semaphore_signal(barrier, inc=1, device_id=dev, device_id_type=MESH)
    pl.semaphore_wait(barrier, len(peers))

    h_r = [rcopy(h_ref.at[:, pl.ds(c * CH, CH)], hz.at[c, 1], hs_s.at[c, 0], hr_s.at[c, 0], right) for c in range(NC)]
    h_l = [rcopy(h_ref.at[:, pl.ds(c * CH, CH)], hz.at[c, 2], hs_s.at[c, 1], hr_s.at[c, 1], left) for c in range(NC)]
    f_r = [rcopy(hz.at[c, 1, pl.ds(0, HR)], hz.at[c, 3, pl.ds(0, HR)], fs_s.at[c, 0], fr_s.at[c, 0], right) for c in range(NC)]
    f_l = [rcopy(hz.at[c, 2, pl.ds(HR, HR)], hz.at[c, 3, pl.ds(HR, HR)], fs_s.at[c, 1], fr_s.at[c, 1], left) for c in range(NC)]
    dk_x = [
        rcopy(g_refs[a].at[sl[s], 1 - z], dk.at[1, s, :, pl.ds(a * HC, HC)], dks_s.at[s, a], dkr_s.at[s, a], pair)
        for s in range(4) for a in range(2)
    ]
    w_x = [
        rcopy(wp.at[c, 0, pl.ds(o, n)], wp.at[c, 1, pl.ds(o, n)], ws_s.at[q], wr_s.at[q], pair)
        for q, (c, o, n) in enumerate(PIECES)
    ]
    g_x = [rcopy(gsend.at[c], grecv.at[c], gs_s.at[c], gr_s.at[c], pair) for c in range(NC)]
    t1_r, t1_l, t2_r, t2_l = [], [], [], []
    for q, (c, o, n) in enumerate(PIECES):
        cols = pl.ds(o, n)
        t1_r.append(rcopy(ts.at[c, 3, pl.ds(0, HR), cols], trh.at[c, 0, :, cols], t1s_s.at[q, 0], t1r_s.at[q, 0], right))
        t1_l.append(rcopy(ts.at[c, 3, pl.ds(HR, HR), cols], trh.at[c, 1, :, cols], t1s_s.at[q, 1], t1r_s.at[q, 1], left))
        t2_r.append(rcopy(ts.at[c, 2, :, cols], trf.at[c, 0, :, cols], t2s_s.at[q, 0], t2r_s.at[q, 0], right))
        t2_l.append(rcopy(ts.at[c, 1, :, cols], trf.at[c, 1, :, cols], t2s_s.at[q, 1], t2r_s.at[q, 1], left))

    def send_h(c):
        h_r[c].start()
        h_l[c].start()

    def convert_w(c):
        for cp in w_loc[c]:
            cp.wait()

        @pl.loop(0, CH // 256)
        def _(i):
            rows = pl.ds(i * 256, 256)
            for a in range(2):
                wp[c, 0, rows, pl.ds(a * HC, HC)] = wcv[c % 2, a, rows].astype(bf16)

        if c + 2 < NC:
            for cp in w_loc[c + 2]:
                cp.start()

    def forward_h(c):
        h_r[c].wait_recv()
        f_r[c].start()
        h_l[c].wait_recv()
        f_l[c].start()

    def grads(c):
        h_loc[c].wait()
        f_r[c].wait_recv()
        f_l[c].wait_recv()

        @pl.loop(0, CH // 256)
        def _(i):
            cols = pl.ds(pl.multiple_of(i * 256, 256), 256)
            rows = pl.ds(i * 256, 256)
            lhs = hz[c, :, :, cols].reshape(4 * RB, 256).T
            gsend[c, rows] = dot_nn(lhs, dk[1].reshape(4 * RB, 2 * HC)).astype(bf16)
            gown[c, rows] = dot_nn(lhs, dk[0].reshape(4 * RB, 2 * HC))

    def produce(c):
        for p in range(2):
            add = dot_nn(hz[c].reshape(4 * RB, CH), wp[c, p]).reshape(4, RB, 2 * HC)
            if c == 0:
                kacc[p] = add
            elif c < NC - 1:
                kacc[p] = kacc[p] + add
            else:
                kst[p] = (kacc[p] + add).astype(bf16)

    def terms_first(q):
        c, o, n = PIECES[q]
        w_x[q].wait_recv()

        @pl.loop(0, n // 256)
        def _(i):
            cols = pl.ds(pl.multiple_of(o + i * 256, 256), 256)
            rows = pl.ds(pl.multiple_of(o + i * 256, 256), 256)
            total = dot_nt(dk[0].reshape(4 * RB, 2 * HC), wp[c, 0, rows])
            total = total + dot_nt(dk[1].reshape(4 * RB, 2 * HC), wp[c, 1, rows])
            ts[c, :, :, cols] = total.astype(bf16).reshape(4, RB, 256)

        t1_r[q].start()
        t1_l[q].start()

    def terms_second(q):
        c, o, n = PIECES[q]
        cols = pl.ds(o, n)
        low, high = pl.ds(0, HR), pl.ds(HR, HR)
        t1_r[q].wait_recv()
        ts[c, 2, low, cols] = (ts[c, 2, low, cols].astype(f32) + trh[c, 0, :, cols].astype(f32)).astype(bf16)
        t2_r[q].start()
        t1_l[q].wait_recv()
        ts[c, 1, high, cols] = (ts[c, 1, high, cols].astype(f32) + trh[c, 1, :, cols].astype(f32)).astype(bf16)
        t2_l[q].start()

    ig_cp = [
        lcopy(ts.at[c, 0, :, pl.ds(o, n)], ig_o.at[:, pl.ds(c * CH + o, n)], ig_s.at[q])
        for q, (c, o, n) in enumerate(PIECES)
    ]

    def terms_last(q):
        c, o, n = PIECES[q]
        cols = pl.ds(o, n)
        t2_r[q].wait_recv()
        t2_l[q].wait_recv()
        total = ts[c, 0, :, cols].astype(f32) + trf[c, 0, :, cols].astype(f32)
        ts[c, 0, :, cols] = (total + trf[c, 1, :, cols].astype(f32)).astype(bf16)
        ig_cp[q].start()

    first_scale = 1.0 / (1.0 - beta_one**step_count)
    second_scale = 1.0 / (1.0 - beta_two**step_count)

    def adam(c):
        g_x[c].wait()
        for cp in ad_loc[c]:
            cp.wait()

        @pl.loop(0, CH // 64)
        def _(i):
            rows = pl.ds(i * 64, 64)
            for a in range(2):
                cols = pl.ds(a * HC, HC)
                g = gown[c, rows, cols] + grecv[c, rows, cols].astype(f32)
                weight = adin[c % 2, 0, a, rows]
                moment = beta_one * adin[c % 2, 1, a, rows] + (1.0 - beta_one) * g
                second = beta_two * adin[c % 2, 2, a, rows] + (1.0 - beta_two) * g * g
                step = (moment * first_scale) / (jnp.sqrt(second * second_scale) + epsilon)
                new = weight - learn_rate * (step + decay_rate * weight)
                gown[c, rows, cols] = new
                gsend[c, rows, cols] = new.astype(bf16)

        if c + 2 < NC:
            for cp in ad_loc[c + 2]:
                cp.start()
        ad_cp[c].start()

        @pl.loop(0, CH // 256)
        def _(i):
            rows = pl.ds(i * 256, 256)
            tile = dot_nt(st[...], gsend[c, rows]).astype(bf16)
            pan[c, 2 * i] = tile[:, :HC]
            pan[c, 2 * i + 1] = tile[:, HC:]

    groups = ((0, 3), (3, 2))

    def chunks(g):
        return pl.ds(groups[g][0], groups[g][1])

    def pan_x(g):
        return [
            rcopy(
                pan.at[chunks(g), pl.ds(lax.rem(x + k, 4) * 2, 2)], prx.at[chunks(g), k - 1],
                px_s.at[g, k], px_r.at[g, k], (r, lax.rem(x + k, 4) * 2 + z),
            )
            for k in range(1, 4)
        ]

    def pan_z(g):
        return [rcopy(psend.at[chunks(g)], prz.at[chunks(g)], pz_s.at[g], pz_r.at[g], pair)]

    def quad_x(g):
        part = quads[g].at[:, zl, core]
        return [rcopy(part, part, qs_s.at[g, k], qr_s.at[g, k], near[k]) for k in range(3)]

    def quad_r(g):
        from_at = ((zl, 1 - core), (1 - zl, core), (1 - zl, 1 - core))
        return [
            rcopy(quads[g].at[:, a, b], quads[g].at[:, a, b], qs_s.at[g, k], qr_s.at[g, k], near[k])
            for k, (a, b) in enumerate(from_at)
        ]

    def y_x(g):
        return [
            rcopy(
                ysends[g].at[k - 1], yalls[g].at[k], ys_s.at[g, k], yr_s.at[g, k],
                (lax.rem(r + 4 * k, 16), t),
            )
            for k in range(1, 4)
        ]

    mine = pl.ds(pl.multiple_of(t * HC, HC), HC)

    def both(at):
        return pl.ds(pl.multiple_of(at * 2 * HC, 2 * HC), 2 * HC)

    def diff_z(g):
        part = dfull.at[chunks(g), :, mine]
        return [rcopy(part, part, dz_s.at[g], dz_r.at[g], pair)]

    def diff_zr(g):
        part = dfull.at[chunks(g), :, pl.ds(pl.multiple_of((x * 2 + 1 - z) * HC, HC), HC)]
        return [rcopy(part, part, dz_s.at[g], dz_r.at[g], pair)]

    def diff_x(g):
        part = dfull.at[chunks(g), :, both(x)]
        return [
            rcopy(part, part, dx_s.at[g, k], dx_r.at[g, k], (r, lax.rem(x + k, 4) * 2 + z))
            for k in range(1, 4)
        ]

    def diff_xr(g):
        out = []
        for k in range(1, 4):
            part = dfull.at[chunks(g), :, both(lax.rem(x + 4 - k, 4))]
            out.append(rcopy(part, part, dx_s.at[g, k], dx_r.at[g, k], (r, lax.rem(x + k, 4) * 2 + z)))
        return out

    def start(cps):
        for cp in cps:
            cp.start()

    def arrived(cps):
        for cp in cps:
            cp.wait_recv()

    def panel_x(g):
        start(pan_x(g))

    def panel_z(g):
        arrived(pan_x(g))
        first, count = groups[g]
        for c in range(first, first + count):
            total = pan[c, x * 2 + 1 - z].astype(f32)
            for k in range(3):
                total = total + prx[c, k, 1 - z].astype(f32)
            psend[c] = total.astype(bf16)
        start(pan_z(g))

    def slab_near(g):
        arrived(pan_z(g))
        first, count = groups[g]
        for c in range(first, first + count):
            total = pan[c, t].astype(f32) + prz[c].astype(f32)
            for k in range(3):
                total = total + prx[c, k, z].astype(f32)
            quads[g][c - first, zl, core] = total.astype(bf16)
        start(quad_x(g))

    def pick(g, n, who):
        other = partner_ref[who]
        return [quads[g][c, lax.rem(other // 2, 2), lax.rem(other, 2)] for c in range(n)]

    def slab_far(g, n):
        arrived(quad_r(g))
        for k in range(1, 4):
            for c, value in enumerate(pick(g, n, lax.rem(r + 4 * k, 16))):
                ysends[g][k - 1, c] = value
        start(y_x(g))
        for c, value in enumerate(pick(g, n, r)):
            yalls[g][0, c] = value

    away = lax.rem(y - partner_ref[r] // 4 + 4, 4)

    def diff_near(g):
        arrived(y_x(g))
        first, count = groups[g]
        for c in range(count):
            own = quads[g][c, zl, core].astype(f32)
            dfull[first + c, :, mine] = (own - yalls[g][away, c].astype(f32)).astype(bf16)
        start(diff_z(g))

    def diff_far(g):
        arrived(diff_zr(g))
        start(diff_x(g))

    def gram_side(g):
        arrived(diff_xr(g))
        first, count = groups[g]
        for c in range(first, first + count):
            d = dfull[c]
            gram = dot_nt(d, d)
            side = dot_nn(d, gsend[c])
            if c == 0:
                gacc[...] = gram
                sacc[...] = side
            else:
                gacc[...] = gacc[...] + gram
                sacc[...] = sacc[...] + side

    def side_near():
        quad2[0, zl, core, pl.ds(0, 32)] = sacc[pl.ds(0, 32), pl.ds(0, HC)].astype(bf16)
        quad2[0, zl, core, pl.ds(32, 32)] = sacc[pl.ds(32, 32), pl.ds(HC, HC)].astype(bf16)
        start(quad_x(2))

    def inverses(mats):
        row_at = lax.broadcasted_iota(jnp.int32, (32, 32), 0)
        col_at = lax.broadcasted_iota(jnp.int32, (32, 32), 1)
        for k in range(32):
            step = []
            for m in mats:
                inv = 1.0 / m[k : k + 1, k : k + 1]
                row = jnp.where(col_at[:1] == k, inv, m[k : k + 1] * inv)
                col = m[:, k : k + 1]
                step.append(jnp.where(row_at == k, row, jnp.where(col_at == k, 0.0, m) - col * row))
            mats = step
        return mats

    def gram_inverses():
        return inverses([gacc[pl.ds(0, 32), pl.ds(0, 32)], gacc[pl.ds(32, 32), pl.ds(32, 32)]])

    def solve(inv):
        arrived(y_x(2))
        other = yall2[away, 0].astype(f32)
        xs[...] = jnp.zeros_like(xs)
        for a in range(2):
            rows, cols = pl.ds(a * 32, 32), pl.ds(a * HC, HC)
            total = sacc[rows, cols] + other[a * 32 : a * 32 + 32]
            xs[rows, cols] = 0.5 * lax.dot_general(
                inv[a], total, (((1,), (0,)), ((), ())),
                precision=lax.Precision.HIGHEST, preferred_element_type=f32,
            )
        xs_cp.start()

    ad_cp = [lcopy(gown.at[c], ad_o.at[c], out_s.at[NC + c]) for c in range(NC)]
    df_cp = lcopy(dfull, df_o, out_s.at[2 * NC])
    xs_cp = lcopy(xs, xs_o, out_s.at[2 * NC + 1])

    send_h(0)
    for cp in dk_x:
        cp.start()
    send_h(1)
    convert_w(0)
    w_x[0].start()
    for c in (0, 1):
        for cp in ad_loc[c]:
            cp.start()

    def arrive(c):
        forward_h(c)
        if c + 2 < NC:
            send_h(c + 2)
        if c + 1 < NC:
            convert_w(c + 1)
        if c == 0:
            for cp in dk_loc:
                cp.wait()
            for cp in dk_x:
                cp.wait_recv()
        grads(c)

    ko = []
    kx = []
    for s in range(4):
        for a in range(2):
            o = (keys_o, vals_o)[a].at[sl[s], z]
            kx.append(rcopy(kst.at[1, s, :, pl.ds(a * HC, HC)], o, ks_s.at[s, a], kr_s.at[s, a], pair))
            ko.append(lcopy(kst.at[0, s, :, pl.ds(a * HC, HC)], o, ko_s.at[s, a]))

    def keys_send(first, last):
        for cp in kx[first:last] + ko[first:last]:
            cp.start()

    arrive(0)
    g_x[0].start()
    arrive(1)
    g_x[1].start()
    w_x[1].start()
    adam(0)
    arrive(2)
    g_x[2].start()
    adam(1)
    arrive(3)
    g_x[3].start()
    w_x[2].start()
    terms_first(0)
    arrive(4)
    g_x[4].start()
    terms_second(0)
    terms_first(1)
    adam(2)
    panel_x(0)
    produce(0)
    terms_second(1)
    terms_last(0)
    adam(3)
    produce(1)
    panel_z(0)
    w_x[3].start()
    terms_first(2)
    terms_last(1)
    terms_second(2)
    produce(2)
    adam(4)
    panel_x(1)
    slab_near(0)
    terms_last(2)
    panel_z(1)
    terms_first(3)
    slab_near(1)
    w_x[4].start()
    w_x[5].start()
    slab_far(0, 3)
    slab_far(1, 2)
    diff_near(0)
    terms_second(3)
    diff_near(1)
    produce(3)
    terms_first(4)
    diff_far(0)
    diff_far(1)
    terms_first(5)
    terms_second(4)
    produce(4)
    terms_last(3)
    gram_side(0)
    gram_side(1)
    df_cp.start()
    side_near()
    keys_send(0, 8)
    terms_second(5)
    inv = gram_inverses()
    slab_far(2, 1)
    terms_last(4)
    solve(inv)
    terms_last(5)

    for cps in (h_r, h_l, f_r, f_l, dk_x, w_x, t1_r, t1_l, t2_r, t2_l, kx):
        for cp in cps:
            cp.wait_send()
    for cp in kx:
        cp.wait_recv()
    for cp in ko:
        cp.wait()
    for cp in ig_cp + ad_cp + [df_cp, xs_cp]:
        cp.wait()

    for g in range(2):
        for cps in (pan_x(g), pan_z(g), diff_z(g), diff_x(g)):
            for cp in cps:
                cp.wait_send()
    for g in range(3):
        for cp in quad_x(g) + y_x(g):
            cp.wait_send()


def gossip_round(h, wk, wv, mk, mv, sk, sv, gk, gv, start, partner):
    dma = pltpu.SemaphoreType.DMA
    any_spec = pl.BlockSpec(memory_space=pl.ANY)
    shapes = (
        jax.ShapeDtypeStruct((4, 2, RB, HC), bf16),
        jax.ShapeDtypeStruct((4, 2, RB, HC), bf16),
        jax.ShapeDtypeStruct((RB, NC * CH), bf16),
        jax.ShapeDtypeStruct((NC, CH, 2 * HC), f32),
        jax.ShapeDtypeStruct((NC, 64, CH), bf16),
        jax.ShapeDtypeStruct((64, 2 * HC), f32),
    )
    scratch = [
        pltpu.VMEM((NC, 4, RB, CH), bf16),
        pltpu.VMEM((NC, 2, CH, 2 * HC), bf16),
        pltpu.VMEM((2, 4, RB, 2 * HC), bf16),
        pltpu.VMEM((NC, CH, 2 * HC), f32),
        pltpu.VMEM((NC, CH, 2 * HC), bf16),
        pltpu.VMEM((NC, CH, 2 * HC), bf16),
        pltpu.VMEM((2, 2, CH, HC), f32),
        pltpu.VMEM((2, 3, 2, CH, HC), f32),
        pltpu.VMEM((NC, 4, RB, CH), bf16),
        pltpu.VMEM((NC, 2, HR, CH), bf16),
        pltpu.VMEM((NC, 2, RB, CH), bf16),
        pltpu.VMEM((2, 4, RB, 2 * HC), f32),
        pltpu.VMEM((2, 4, RB, 2 * HC), bf16),
        pltpu.VMEM((NC, 8, 64, HC), bf16),
        pltpu.VMEM((NC, 3, 2, 64, HC), bf16),
        pltpu.VMEM((NC, 64, HC), bf16),
        pltpu.VMEM((NC, 64, HC), bf16),
        *[pltpu.VMEM((n, 2, 2, 64, HC), bf16) for n in (3, 2, 1)],
        *[pltpu.VMEM((3, n, 64, HC), bf16) for n in (3, 2, 1)],
        *[pltpu.VMEM((4, n, 64, HC), bf16) for n in (3, 2, 1)],
        pltpu.VMEM((64, 2 * HC), bf16),
        pltpu.VMEM((NC, 64, CH), bf16),
        pltpu.VMEM((64, 64), f32),
        pltpu.VMEM((64, 2 * HC), f32),
        pltpu.VMEM((64, 2 * HC), f32),
        dma((NC,)), dma((NC, 2)), dma((NC, 2)), dma((NC, 2)), dma((NC, 2)),
        dma((4, 2)), dma((4, 2)), dma((4, 2)), dma((2, 2)), dma((NP,)), dma((NP,)),
        dma((NC,)), dma((NC,)), dma((2, 3, 2)),
        dma((NP, 2)), dma((NP, 2)), dma((NP, 2)), dma((NP, 2)), dma((NP,)),
        dma((4, 2)), dma((4, 2)), dma((4, 2)), dma((2 * NC + 2,)),
        dma((2, 4)), dma((2, 4)), dma((2,)), dma((2,)), dma((3, 3)), dma((3, 3)),
        dma((3, 4)), dma((3, 4)), dma((2,)), dma((2,)), dma((2, 4)), dma((2, 4)),
    ]
    return pl.pallas_call(
        round_kernel,
        out_shape=shapes,
        in_specs=[any_spec] * 9
        + [pl.BlockSpec(memory_space=pltpu.VMEM), pl.BlockSpec(memory_space=pltpu.SMEM)],
        out_specs=[any_spec] * 6,
        scratch_shapes=scratch,
        compiler_params=pltpu.CompilerParams(
            collective_id=0, has_side_effects=True, vmem_limit_bytes=60 << 20
        ),
        cost_estimate=pl.CostEstimate(flops=13_000_000_000, bytes_accessed=60_000_000, transcendentals=0),
        name="gossip_round",
    )(h, wk, wv, mk, mv, sk, sv, gk, gv, start, partner)


def renew_kernel(k_ref, v_ref, i_ref, ad_ref, df_ref, x_ref, k_o, v_o, i_o, nk_o, nv_o):
    k_o[...] = k_ref[...]
    v_o[...] = v_ref[...]
    i_o[...] = i_ref[...]
    high = x_ref[...].astype(bf16)
    low = (x_ref[...] - high.astype(f32)).astype(bf16)

    @pl.loop(0, CH // 256)
    def _(i):
        cols = pl.ds(pl.multiple_of(i * 256, 256), 256)
        rows = pl.ds(i * 256, 256)
        lhs = df_ref[0, :, cols].T
        new = ad_ref[0, rows] - (dot_nn(lhs, high) + dot_nn(lhs, low))
        nk_o[0, rows] = new[:, :HC]
        nv_o[0, rows] = new[:, HC:]


def renew(keys, values, input_grad, adapted, diff, panels):
    kv_spec = pl.BlockSpec((2 * RB, HC), lambda c: (jnp.minimum(c, 3), 0))
    new_spec = pl.BlockSpec((1, CH, HC), lambda c: (0, c, 0))
    ig_spec = pl.BlockSpec((RB, CH), lambda c: (0, c))
    new_shape = jax.ShapeDtypeStruct((1, NC * CH, HC), f32)
    return pl.pallas_call(
        renew_kernel,
        grid=(NC,),
        out_shape=(
            jax.ShapeDtypeStruct(keys.shape, bf16),
            jax.ShapeDtypeStruct(values.shape, bf16),
            jax.ShapeDtypeStruct(input_grad.shape, bf16),
            new_shape, new_shape,
        ),
        in_specs=[kv_spec, kv_spec, ig_spec,
            pl.BlockSpec((1, CH, 2 * HC), lambda c: (c, 0, 0)),
            pl.BlockSpec((1, 64, CH), lambda c: (c, 0, 0)),
            pl.BlockSpec((64, 2 * HC), lambda c: (0, 0)),
        ],
        out_specs=[kv_spec, kv_spec, ig_spec, new_spec, new_spec],
        compiler_params=pltpu.CompilerParams(vmem_limit_bytes=60 << 20),
        cost_estimate=pl.CostEstimate(flops=400_000_000, bytes_accessed=17_000_000, transcendentals=0),
        name="renew",
    )(keys, values, input_grad, adapted, diff, panels)


def body(hidden, w_key, w_value, moment_key, moment_value, second_key, second_value,
         grad_keys, grad_values, seed_panels, partner):
    start = jnp.transpose(seed_panels, (0, 2, 1))
    keys, values, input_grad, adapted, diff, panels = gossip_round(
        hidden, w_key, w_value, moment_key, moment_value, second_key, second_value,
        grad_keys.reshape(4, 2, RB, HC), grad_values.reshape(4, 2, RB, HC), start, partner,
    )
    keys, values, input_grad, new_key, new_value = renew(
        keys.reshape(8 * RB, HC), values.reshape(8 * RB, HC), input_grad, adapted, diff, panels
    )
    return keys, values, input_grad, new_key, new_value


def solution(mesh):
    return jax.shard_map(
        body,
        mesh=mesh,
        in_specs=(
            P(("replica", "tensor"), None),
            P("replica", None, "tensor"),
            P("replica", None, "tensor"),
            P("replica", None, "tensor"),
            P("replica", None, "tensor"),
            P("replica", None, "tensor"),
            P("replica", None, "tensor"),
            P("replica", "tensor"),
            P("replica", "tensor"),
            P(None, "tensor", None),
            P(),
        ),
        out_specs=(
            P("replica", "tensor"),
            P("replica", "tensor"),
            P(("replica", "tensor"), None),
            P("replica", None, "tensor"),
            P("replica", None, "tensor"),
        ),
        check_vma=False,
    )
```
